32 devices in a mesh: stn: 16 (over z, y, x), tm: 2 (over core).
Axes of the slice: x: 2, y: 2, z: 4, core: 2. Of those that a mesh axis runs over, the one named last changes fastest.
Arguments:
- voltages: bfloat16 [128, 256, 4096], P('stn', 'tm'), may hold values from -6 to 6
- filter_taps: float32 [16, 4096], replicated, may hold values from -1.5 to 1.5
- channel_keep: int32 [256], replicated, may hold values from 0 to 1, as said below
- station_order: int32 [64], replicated, may hold values from 0 to 63, each once
Outputs:
- visibilities: float32 [128, 16, 2, 128], P('tm', 'stn')
The draws below stay inside these ranges and needn't reach their ends.
Inputs may be any that keep to these rules, and one draw needn't show every extreme that they name: `channel_keep`: exactly 16 entries are 1. `station_order`: a permutation of the stations.
All inputs are finite; a program needn't handle non-finite values.
Results may differ from the reference program's by a relative error of at most 0.0039.
Values may be sent and summed in bfloat16 or wider, within the bound.
A program may use at most 64 MiB of HBM per device.

```python
import math
import jax
import jax.numpy as jnp
from jax import lax

ST_DEV = 4
STATIONS = 64
INPUTS = 128
NCHAN = 4096
SUB = 256
SUB_LO = 1024
TAPS = 16
KEPT = 16
FRAMES = 256
N_STN = 16


def draw_channel_keep(key, part):
    order = jax.random.permutation(key, SUB)
    return (order < KEPT).astype(jnp.int32)


def steps_of(rng, extent, cuts, low, top_value):
    gain = 1.0
    for dim, parts in cuts:
        steps = jax.random.uniform(jax.random.fold_in(jax.random.fold_in(rng, 6), dim), (parts,), jnp.float32, low / len(cuts), top_value / len(cuts))
        gain = gain * jnp.repeat(jnp.exp(steps), extent[dim] // parts).reshape((-1,) + (1,) * (len(extent) - 1 - dim))
    return gain


def normal_values(key, extent, spread, limit, split=(), kind=jnp.bfloat16):
    result = jax.random.normal(key, extent, jnp.float32) * spread
    if len(split) > 0:
        result = steps_of(key, extent, split, -0.22, 0.18) * result
    return jnp.clip(result, min=-limit, max=limit).astype(kind)


def setup_inputs(seed: int = 0) -> dict:
    keys = jax.random.split(jax.random.key(seed), 5)
    voltages = normal_values(keys[0], (INPUTS, FRAMES, NCHAN), 1.0, 6.0, ((0, 16), (1, 2)))
    filter_taps = normal_values(keys[1], (TAPS, NCHAN), TAPS ** -0.5, 1.5, (), jnp.float32)
    channel_keep = draw_channel_keep(jax.random.fold_in(keys[4], 71), 0)
    station_order = jax.random.permutation(keys[3], STATIONS).astype(jnp.int32)
    return {"voltages": voltages, "filter_taps": filter_taps, "channel_keep": channel_keep, "station_order": station_order}


def dft_rows(n_chan, n_sub, sub_first):
    sample_idx = jnp.arange(n_chan, dtype=jnp.int32)
    channel_idx = jnp.arange(n_sub, dtype=jnp.int32) + sub_first
    product = channel_idx[:, None] * sample_idx[None, :] % n_chan
    phase = 2.0 * math.pi / n_chan * product.astype(jnp.float32)
    norm_factor = 1.0 / math.sqrt(n_chan)
    return (jnp.stack([jnp.cos(phase), -jnp.sin(phase)]) * norm_factor).astype(jnp.bfloat16)

def keep_matrix(channel_keep, kept_total):
    position = jnp.cumsum(channel_keep) - 1
    slots = jnp.arange(kept_total, dtype=jnp.int32)
    matches = (position[:, None] == slots[None, :]) & (channel_keep[:, None] == 1)
    return matches.astype(jnp.float32)

def reference(voltages, filter_taps, channel_keep, station_order):
    history_len = TAPS - 1
    dft_table = dft_rows(NCHAN, SUB, SUB_LO)
    selector = keep_matrix(channel_keep, KEPT)
    kept_table = jnp.einsum('ck,pcn->pkn', selector, dft_table.astype(jnp.float32)).astype(jnp.bfloat16)
    kept_float = kept_table.astype(jnp.float32)
    blocks = voltages.reshape(N_STN, 2 * ST_DEV, FRAMES, NCHAN)
    taps_float = filter_taps.astype(jnp.float32)

    def channelize(block_volts):
        padded = jnp.concatenate([jnp.zeros((block_volts.shape[0], history_len, NCHAN), jnp.bfloat16), block_volts], axis=1).astype(jnp.float32)
        filtered = jnp.zeros((block_volts.shape[0], FRAMES, NCHAN), jnp.float32)
        for tap_index in range(TAPS):
            filtered = filtered + taps_float[tap_index][None, None, :] * padded[:, tap_index:tap_index + FRAMES, :]
        filtered = filtered.astype(jnp.bfloat16).astype(jnp.float32)
        return jnp.einsum('pkn,ifn->kipf', kept_float, filtered).astype(jnp.bfloat16)
    per_block = lax.map(channelize, blocks)
    spectra = jnp.transpose(per_block, (1, 0, 2, 3, 4)).reshape(KEPT, INPUTS, 2, FRAMES)
    row_ids = jnp.arange(INPUTS, dtype=jnp.int32)
    targets = 2 * station_order[row_ids // 2] + row_ids % 2
    catalog = jnp.zeros_like(spectra).at[:, targets].set(spectra)

    def correlate(channel_spec):
        values = channel_spec.astype(jnp.float32)
        real_part = jnp.einsum('ipf,jpf->ij', values, values)
        imag_part = jnp.einsum('if,jf->ij', values[:, 1], values[:, 0]) - jnp.einsum('if,jf->ij', values[:, 0], values[:, 1])
        return jnp.stack([real_part, imag_part]) * (1.0 / FRAMES)
    sums = lax.map(correlate, catalog)
    return jnp.transpose(sums, (2, 0, 1, 3))
```

```python
import functools
import math

import jax
import jax.numpy as jnp
from jax import lax
from jax.experimental import pallas as pl
from jax.experimental.pallas import tpu as pltpu
from jax.sharding import PartitionSpec as P

SUB_LO = 1024
CH_DEV = 1
GROUP = 16
CHUNK = 512
MESH = pl.DeviceIdType.MESH


def fused_kernel(
    volt_hbm, taps_hbm, keep_hbm, order_hbm, out_ref, volt_ref, taps_ref, keep_ref, order_ref,
    acc_ref, base_ref, chan_ref, even_ref, odd_ref, main_ref, tail_ref, before_ref, spectra_ref, all_ref, catalog_ref,
    sems, load_sems, *, groups, stations,
):
    group = pl.program_id(0)
    step = pl.program_id(1)
    steps = pl.num_programs(1)
    inputs, frames, wide = volt_ref.shape[1:]
    n_taps, n_chan = taps_ref.shape
    n_sub = keep_ref.shape[1]
    unit = 2.0 * math.pi / n_chan
    rows = 2 * GROUP
    stn = lax.axis_index("stn")
    tm = lax.axis_index("tm")
    devices = groups * stations
    me = stn * groups + tm
    barrier = pltpu.get_barrier_semaphore()

    def there(distance):
        device = lax.rem(me + distance, devices)
        return device // groups, lax.rem(device, groups)

    def load(part):
        columns = pl.ds(pl.multiple_of(part * wide, wide), wide)
        return pltpu.make_async_copy(volt_hbm.at[:, :, columns], volt_ref.at[part], load_sems.at[3 + part])

    order_copy = pltpu.make_async_copy(order_hbm, order_ref, load_sems.at[0])

    @pl.when((group == 0) & (step == 0))
    def _():
        keep_copy = pltpu.make_async_copy(keep_hbm, keep_ref, load_sems.at[1])
        taps_copy = pltpu.make_async_copy(taps_hbm, taps_ref, load_sems.at[2])
        keep_copy.start()
        taps_copy.start()
        for part in range(n_chan // wide):
            load(part).start()
        order_copy.start()

        @pl.loop(1, devices)
        def _(distance):
            pl.semaphore_signal(barrier, inc=1, device_id=there(distance), device_id_type=MESH)

        keep_copy.wait()
        taps_copy.wait()

    def weigh(w_ref, part):
        angle = ((chan_ref[...] * (part * CHUNK)) % n_chan).astype(jnp.float32) * unit
        norm = 1.0 / math.sqrt(n_chan)
        cos_step = (jnp.cos(angle) * norm)[:, :1]
        sin_step = (jnp.sin(angle) * norm)[:, :1]
        cos_base = base_ref[0]
        sin_base = base_ref[1]
        real = cos_step * cos_base - sin_step * sin_base
        imag = -(sin_step * cos_base + cos_step * sin_base)
        table = jnp.concatenate([real, imag], axis=0).astype(jnp.bfloat16).astype(jnp.float32)
        taps = taps_ref[:, pl.ds(pl.multiple_of(part * CHUNK, CHUNK), CHUNK)]
        for tap in range(n_taps):
            w_ref[tap * rows:(tap + 1) * rows, :] = (table * taps[tap:tap + 1, :]).astype(jnp.bfloat16)

    @pl.when(step == 0)
    def _():
        keep = keep_ref[...]
        before = lax.broadcasted_iota(jnp.int32, (n_sub, n_sub), 0) <= lax.broadcasted_iota(jnp.int32, (n_sub, n_sub), 1)
        keep_rows = jnp.broadcast_to(keep, (GROUP, n_sub))
        rank = jnp.dot(
            keep_rows.astype(jnp.float32).astype(jnp.bfloat16),
            before.astype(jnp.float32).astype(jnp.bfloat16),
            preferred_element_type=jnp.float32,
        )
        slot = (lax.broadcasted_iota(jnp.int32, (GROUP, n_sub), 0) + 1 + group * GROUP).astype(jnp.float32)
        number = lax.broadcasted_iota(jnp.int32, (GROUP, n_sub), 1).astype(jnp.float32)
        hit = jnp.where((rank == slot) & (keep_rows == 1), number, 0.0)
        channel = jnp.sum(hit, axis=1, keepdims=True).astype(jnp.int32) + SUB_LO
        chan_ref[...] = jnp.broadcast_to(channel, (GROUP, 128))
        column = lax.broadcasted_iota(jnp.int32, (GROUP, CHUNK), 1)
        angle = ((channel * column) % n_chan).astype(jnp.float32) * unit
        base_ref[0] = jnp.cos(angle)
        base_ref[1] = jnp.sin(angle)
        acc_ref[...] = jnp.zeros_like(acc_ref)
        weigh(even_ref, 0)

    @pl.when(group == 0)
    def _():
        load(step).wait()

    def times(w_ref, half):
        volts = volt_ref[step, :, :, half * CHUNK:(half + 1) * CHUNK].reshape(inputs * frames, CHUNK)
        return lax.dot_general(w_ref[...], volts, (((1,), (1,)), ((), ())), preferred_element_type=jnp.float32)

    weigh(odd_ref, 2 * step + 1)
    acc_ref[...] += times(even_ref, 0)
    weigh(even_ref, lax.rem(2 * step + 2, 2 * steps))
    acc_ref[...] += times(odd_ref, 1)

    @pl.when(step == steps - 1)
    def _():
        lane = lax.broadcasted_iota(jnp.int32, (rows, frames), 1)
        for i in range(inputs):
            inside = jnp.zeros((rows, frames), jnp.float32)
            beyond = jnp.zeros((rows, frames), jnp.float32)
            for tap in range(n_taps):
                shift = n_taps - 1 - tap
                piece = acc_ref[tap * rows:(tap + 1) * rows, i * frames:(i + 1) * frames]
                if shift > 0:
                    piece = pltpu.roll(piece, shift, axis=1)
                    beyond = beyond + jnp.where(lane < shift, piece, 0.0)
                    piece = jnp.where(lane < shift, 0.0, piece)
                inside = inside + piece
            for p in range(2):
                place = pl.ds(group * (GROUP * 2 * inputs) + p * inputs + i, GROUP, stride=2 * inputs)
                main_ref[place, :] = inside[p * GROUP:(p + 1) * GROUP]
                tail_ref[place, :] = beyond[p * GROUP:(p + 1) * GROUP]

    @pl.when((group == pl.num_programs(0) - 1) & (step == steps - 1))
    def _():
        pl.semaphore_wait(barrier, devices - 1)
        tail_copy = pltpu.make_async_remote_copy(
            src_ref=tail_ref,
            dst_ref=before_ref,
            send_sem=sems.at[0],
            recv_sem=sems.at[1],
            device_id=(stn, lax.rem(tm + 1, groups)),
            device_id_type=MESH,
        )
        tail_copy.start()
        order_copy.wait()

        tile = 2 * inputs
        total = stations * inputs
        half = order_ref.shape[1]
        cols = stations * tile
        row = lax.broadcasted_iota(jnp.int32, (total, half), 0)
        at_station = jnp.where(order_ref[...] == row // 2, 1.0, 0.0).astype(jnp.bfloat16)
        col = lax.broadcasted_iota(jnp.int32, (half, cols), 1)
        station = (col // tile) * (inputs // 2) + (col % inputs) // 2
        spread = jnp.where(station == lax.broadcasted_iota(jnp.int32, (half, cols), 0), 1.0, 0.0).astype(jnp.bfloat16)
        chosen = jnp.dot(at_station, spread, preferred_element_type=jnp.float32)
        row = lax.broadcasted_iota(jnp.int32, (total, cols), 0)
        col = lax.broadcasted_iota(jnp.int32, (total, cols), 1)
        chosen = jnp.where(row % 2 == col % 2, chosen, 0.0)
        side = (col // inputs) % 2
        pick = [jnp.where(side == p, chosen, 0.0).astype(jnp.bfloat16) for p in range(2)]

        tail_copy.wait()
        history = jnp.where(tm > 0, before_ref[...], 0.0)
        spectra_ref[...] = (main_ref[...] + history).astype(jnp.bfloat16).reshape(spectra_ref.shape)

        place = tm * stations + stn
        own = pltpu.make_async_copy(spectra_ref.at[stn], all_ref.at[place], sems.at[2])
        own.start()

        @pl.loop(1, devices)
        def _(distance):
            to = there(distance)
            pltpu.make_async_remote_copy(
                src_ref=spectra_ref.at[to[0]],
                dst_ref=all_ref.at[place],
                send_sem=sems.at[3],
                recv_sem=sems.at[4],
                device_id=to,
                device_id_type=MESH,
            ).start()

        own.wait()
        others = all_ref.at[pl.ds(0, devices - 1)]
        pltpu.make_async_remote_copy(
            src_ref=others,
            dst_ref=others,
            send_sem=sems.at[3],
            recv_sem=sems.at[4],
            device_id=there(1),
            device_id_type=MESH,
        ).wait()

        for g in range(groups):
            tiles = all_ref[g * stations:(g + 1) * stations].reshape(cols, frames)
            for p in range(2):
                found = jnp.dot(pick[p], tiles, preferred_element_type=jnp.float32)
                catalog_ref[p, :, g * frames:(g + 1) * frames] = found.astype(jnp.bfloat16)
        count = total // groups
        mine = pl.ds(pl.multiple_of(tm * count, count), count)
        scale = 1.0 / (groups * frames)

        def product(p, q):
            return lax.dot_general(
                catalog_ref[p, mine, :], catalog_ref[q], (((1,), (1,)), ((), ())), preferred_element_type=jnp.float32
            )

        out_ref[:, 0, :] = (product(0, 0) + product(1, 1)) * scale
        out_ref[:, 1, :] = (product(1, 0) - product(0, 1)) * scale


def body(voltages, filter_taps, channel_keep, station_order):
    inputs, frames, n_chan = voltages.shape
    n_taps = filter_taps.shape[0]
    n_sub = channel_keep.shape[0]
    half = station_order.shape[0]
    groups = lax.axis_size("tm")
    stations = lax.axis_size("stn")
    kept = CH_DEV * stations
    steps = n_chan // (2 * CHUNK)
    total = stations * inputs
    tile = 2 * inputs
    weights = pltpu.VMEM((2 * GROUP * n_taps, CHUNK), jnp.bfloat16)
    sums = pl.pallas_call(
        functools.partial(fused_kernel, groups=groups, stations=stations),
        grid=(kept // GROUP, steps),
        in_specs=[pl.BlockSpec(memory_space=pltpu.HBM)] * 4,
        out_specs=pl.BlockSpec((total // groups, 2, total), lambda g, j: (0, 0, 0)),
        out_shape=jax.ShapeDtypeStruct((total // groups, 2, total), jnp.float32),
        scratch_shapes=[
            pltpu.VMEM((steps, inputs, frames, 2 * CHUNK), jnp.bfloat16),
            pltpu.VMEM((n_taps, n_chan), jnp.float32),
            pltpu.VMEM((1, n_sub), jnp.int32),
            pltpu.VMEM((1, half), jnp.int32),
            pltpu.VMEM((2 * GROUP * n_taps, inputs * frames), jnp.float32),
            pltpu.VMEM((2, GROUP, CHUNK), jnp.float32),
            pltpu.VMEM((GROUP, 128), jnp.int32),
            weights,
            weights,
            pltpu.VMEM((kept * tile, frames), jnp.float32),
            pltpu.VMEM((kept * tile, frames), jnp.float32),
            pltpu.VMEM((kept * tile, frames), jnp.float32),
            pltpu.VMEM((kept, tile, frames), jnp.bfloat16),
            pltpu.VMEM((groups * stations, tile, frames), jnp.bfloat16),
            pltpu.VMEM((2, total, groups * frames), jnp.bfloat16),
            pltpu.SemaphoreType.DMA((5,)),
            pltpu.SemaphoreType.DMA((3 + steps,)),
        ],
        compiler_params=pltpu.CompilerParams(collective_id=0, has_side_effects=True, vmem_limit_bytes=40 << 20),
    )(*[pltpu.with_memory_space_constraint(x, pltpu.HBM) for x in (voltages, filter_taps, channel_keep.reshape(1, n_sub), station_order.reshape(1, half))])
    return sums.reshape(total // groups, CH_DEV, 2, total)


def solution(mesh):
    placed = (P("stn", "tm", None), P(), P(), P())
    return jax.shard_map(
        body, mesh=mesh, in_specs=placed, out_specs=P("tm", "stn", None, None), check_vma=False
    )
```

```python
import functools
import math

import jax
import jax.numpy as jnp
from jax import lax
from jax.experimental import pallas as pl
from jax.experimental.pallas import tpu as pltpu
from jax.sharding import PartitionSpec as P

SUB_LO = 1024
GROUP = 8
CHUNK = 512
CUTS = (1024, 2048, 3072)
MESH = pl.DeviceIdType.MESH
NT = (((1,), (1,)), ((), ()))


def fused_kernel(
    volt_hbm, taps_hbm, keep_hbm, order_hbm, out_ref, volt_ref, taps_ref, keep_ref, order_ref,
    acc_ref, base_ref, chan_ref, first_ref, later_ref, main_ref, spectra_ref, tails_ref, all_ref, before_ref, catalog_ref,
    sems, load_sems, *, groups, stations,
):
    inputs, frames, n_chan = volt_ref.shape
    n_taps = taps_ref.shape[0]
    n_sub = keep_ref.shape[1]
    unit = 2.0 * math.pi / n_chan
    rows = 2 * GROUP
    turns = stations // GROUP
    span = frames // inputs
    tile = 2 * inputs
    stn = lax.axis_index("stn")
    tm = lax.axis_index("tm")
    devices = groups * stations
    me = stn * groups + tm
    place = tm * stations + stn
    last = groups - 1
    barrier = pltpu.get_barrier_semaphore()
    edges = [0] + [cut for cut in CUTS if cut < n_chan] + [n_chan]
    parts = [slice(lo, hi) for lo, hi in zip(edges[:-1], edges[1:])]

    keep_copy = pltpu.make_async_copy(keep_hbm, keep_ref, load_sems.at[0])
    taps_copy = pltpu.make_async_copy(taps_hbm, taps_ref, load_sems.at[1])
    order_copy = pltpu.make_async_copy(order_hbm, order_ref, load_sems.at[2])
    loads = [
        pltpu.make_async_copy(volt_hbm.at[:, :, part], volt_ref.at[:, :, part], load_sems.at[3 + n])
        for n, part in enumerate(parts)
    ]
    keep_copy.start()
    taps_copy.start()
    for load in loads:
        load.start()
    order_copy.start()

    @pl.loop(1, devices)
    def _(distance):
        device = lax.rem(me + distance, devices)
        pl.semaphore_signal(
            barrier, inc=1, device_id=(device // groups, lax.rem(device, groups)), device_id_type=MESH
        )

    def turn(number):
        return lax.rem(stn // GROUP + 1 + number, turns)

    def channels(numbers):
        keep = keep_ref[...]
        before = lax.broadcasted_iota(jnp.int32, (n_sub, n_sub), 0) <= lax.broadcasted_iota(jnp.int32, (n_sub, n_sub), 1)
        count = GROUP * len(numbers)
        keep_rows = jnp.broadcast_to(keep, (count, n_sub))
        rank = jnp.dot(
            keep_rows.astype(jnp.float32).astype(jnp.bfloat16),
            before.astype(jnp.float32).astype(jnp.bfloat16),
            preferred_element_type=jnp.float32,
        )
        slot = jnp.concatenate(
            [lax.broadcasted_iota(jnp.int32, (GROUP, n_sub), 0) + 1 + turn(number) * GROUP for number in numbers]
        ).astype(jnp.float32)
        number = lax.broadcasted_iota(jnp.int32, (count, n_sub), 1).astype(jnp.float32)
        hit = jnp.where((rank == slot) & (keep_rows == 1), number, 0.0)
        channel = jnp.sum(hit, axis=1, keepdims=True).astype(jnp.int32) + SUB_LO
        chan_ref[0:count] = jnp.broadcast_to(channel, (count, 128))
        column = lax.broadcasted_iota(jnp.int32, (count, CHUNK), 1)
        angle = ((channel * column) % n_chan).astype(jnp.float32) * unit
        base_ref[0, 0:count] = jnp.cos(angle)
        base_ref[1, 0:count] = jnp.sin(angle)

    def weigh(part, targets):
        count = GROUP * len(targets)
        angle = ((chan_ref[0:count] * (part * CHUNK)) % n_chan).astype(jnp.float32) * unit
        norm = 1.0 / math.sqrt(n_chan)
        cos_step = (jnp.cos(angle) * norm)[:, :1]
        sin_step = (jnp.sin(angle) * norm)[:, :1]
        cos_base = base_ref[0, 0:count]
        sin_base = base_ref[1, 0:count]
        real = cos_step * cos_base - sin_step * sin_base
        imag = -(sin_step * cos_base + cos_step * sin_base)
        columns = pl.ds(part * CHUNK, CHUNK) if isinstance(part, int) else pl.ds(pl.multiple_of(part * CHUNK, CHUNK), CHUNK)
        taps = taps_ref[:, columns]
        for n, w_ref in enumerate(targets):
            own = slice(n * GROUP, (n + 1) * GROUP)
            table = jnp.concatenate([real[own], imag[own]], axis=0).astype(jnp.bfloat16).astype(jnp.float32)
            for tap in range(n_taps):
                w_ref[tap * rows:(tap + 1) * rows, columns] = (table * taps[tap:tap + 1, :]).astype(jnp.bfloat16)

    lane = lax.broadcasted_iota(jnp.int32, (rows, frames), 1)

    def combine(number, product):
        packed = jnp.zeros((rows, frames), jnp.float32)
        for pair in range(inputs // 2):
            sums = product(pair)
            for half in range(2):
                i = 2 * pair + half
                inside = sums[(n_taps - 1) * rows:, half * frames:(half + 1) * frames]
                beyond = jnp.zeros((rows, frames), jnp.float32)
                for tap in range(n_taps - 1):
                    shift = n_taps - 1 - tap
                    piece = pltpu.roll(sums[tap * rows:(tap + 1) * rows, half * frames:(half + 1) * frames], shift, axis=1)
                    beyond = beyond + jnp.where(lane < shift, piece, 0.0)
                    inside = inside + jnp.where(lane < shift, 0.0, piece)
                for p in range(2):
                    main_ref[pl.ds(p * inputs + i, GROUP, stride=tile), :] = inside[p * GROUP:(p + 1) * GROUP]
                packed = packed + (pltpu.roll(beyond, frames - i * span, axis=1) if i > 0 else beyond)
        first = turn(number) * GROUP
        spectra_ref[pl.ds(first, GROUP)] = main_ref[...].astype(jnp.bfloat16).reshape(GROUP, tile, frames)
        for p in range(2):
            tails_ref[pl.ds(first, GROUP), p, :] = packed[p * GROUP:(p + 1) * GROUP]

        @pl.loop(0, GROUP * groups)
        def _(distance):
            near = lax.rem(me + 1 + distance, GROUP * groups)
            to_stn = first + near // groups
            to_tm = lax.rem(near, groups)

            @pl.when((to_stn != stn) | (to_tm != tm))
            def _():
                pltpu.make_async_remote_copy(
                    src_ref=spectra_ref.at[to_stn],
                    dst_ref=all_ref.at[place],
                    send_sem=sems.at[0],
                    recv_sem=sems.at[1],
                    device_id=(to_stn, to_tm),
                    device_id_type=MESH,
                ).start()

                @pl.when(tm < last)
                def _():
                    pltpu.make_async_remote_copy(
                        src_ref=tails_ref.at[to_stn],
                        dst_ref=before_ref.at[place],
                        send_sem=sems.at[2],
                        recv_sem=sems.at[3],
                        device_id=(to_stn, to_tm),
                        device_id_type=MESH,
                    ).start()

    keep_copy.wait()
    taps_copy.wait()
    channels((0, 1))
    for part in range(n_chan // CHUNK):
        weigh(part, (first_ref, later_ref))

    def partial(part):
        volts = volt_ref[:, :, part].reshape(inputs * frames, part.stop - part.start)
        return lax.dot_general(first_ref[:, part], volts, NT, preferred_element_type=jnp.float32)

    for n, part in enumerate(parts[:-1]):
        loads[n].wait()
        if n == 0:
            acc_ref[...] = partial(part)
        else:
            acc_ref[...] += partial(part)

    loads[-1].wait()
    pl.semaphore_wait(barrier, devices - 1)

    def first_sums(pair):
        part = parts[-1]
        volts = volt_ref[2 * pair:2 * pair + 2, :, part].reshape(2 * frames, part.stop - part.start)
        found = lax.dot_general(first_ref[:, part], volts, NT, preferred_element_type=jnp.float32)
        return acc_ref[:, 2 * pair * frames:(2 * pair + 2) * frames] + found

    combine(0, first_sums)

    def later_sums(pair):
        volts = volt_ref[2 * pair:2 * pair + 2].reshape(2 * frames, n_chan)
        return lax.dot_general(later_ref[...], volts, NT, preferred_element_type=jnp.float32)

    if turns == 2:
        combine(1, later_sums)
    else:
        @pl.loop(1, turns)
        def _(number):
            @pl.when(number > 1)
            def _():
                channels((number,))

                @pl.loop(0, n_chan // CHUNK)
                def _(part):
                    weigh(part, (later_ref,))

            combine(number, later_sums)

    own = pltpu.make_async_copy(spectra_ref.at[stn], all_ref.at[place], sems.at[4])
    own.start()

    @pl.when(tm < last)
    def _():
        own_tail = pltpu.make_async_copy(tails_ref.at[stn], before_ref.at[place], sems.at[5])
        own_tail.start()
        own_tail.wait()

    order_copy.wait()
    total = stations * inputs
    half = order_ref.shape[1]
    cols = stations * tile
    row = lax.broadcasted_iota(jnp.int32, (total, half), 0)
    at_station = jnp.where(order_ref[...] == row // 2, 1.0, 0.0).astype(jnp.bfloat16)
    col = lax.broadcasted_iota(jnp.int32, (half, cols), 1)
    station = (col // tile) * (inputs // 2) + (col % inputs) // 2
    spread = jnp.where(station == lax.broadcasted_iota(jnp.int32, (half, cols), 0), 1.0, 0.0).astype(jnp.bfloat16)
    chosen = jnp.dot(at_station, spread, preferred_element_type=jnp.float32)
    row = lax.broadcasted_iota(jnp.int32, (total, cols), 0)
    col = lax.broadcasted_iota(jnp.int32, (total, cols), 1)
    chosen = jnp.where(row % 2 == col % 2, chosen, 0.0)
    side = (col // inputs) % 2
    pick = [jnp.where(side == p, chosen, 0.0).astype(jnp.bfloat16) for p in range(2)]

    own.wait()
    others = all_ref.at[pl.ds(0, devices - 1)]
    pltpu.make_async_remote_copy(
        src_ref=others,
        dst_ref=others,
        send_sem=sems.at[0],
        recv_sem=sems.at[1],
        device_id=(stn, lax.rem(tm + 1, groups)),
        device_id_type=MESH,
    ).wait()

    def tails_wait(count, sent):
        ref = tails_all_ref(count)
        copy = pltpu.make_async_remote_copy(
            src_ref=ref,
            dst_ref=ref,
            send_sem=sems.at[2],
            recv_sem=sems.at[3],
            device_id=(stn, lax.rem(tm + 1, groups)),
            device_id_type=MESH,
        )
        if sent:
            copy.wait_send()
        else:
            copy.wait_recv()

    def tails_all_ref(count):
        return before_ref.at[pl.ds(0, count)]

    slots = last * stations

    @pl.when(tm < last)
    def _():
        tails_wait(slots - 1, False)
        tails_wait(devices - 1, True)

    @pl.when(tm == last)
    def _():
        tails_wait(slots, False)

    for g in range(groups):
        tiles = all_ref[g * stations:(g + 1) * stations].reshape(cols, frames)
        if g > 0:
            tails = before_ref[(g - 1) * stations:g * stations].reshape(2 * stations, 1, frames)
            tails = jnp.broadcast_to(tails, (2 * stations, inputs, frames)).reshape(cols, frames)
            tails = pltpu.roll(tails, 0, axis=1, stride=span, stride_axis=0)
            early = lax.broadcasted_iota(jnp.int32, (cols, frames), 1) < n_taps - 1
            tiles = (tiles.astype(jnp.float32) + jnp.where(early, tails, 0.0)).astype(jnp.bfloat16)
        for p in range(2):
            found = jnp.dot(pick[p], tiles, preferred_element_type=jnp.float32)
            at = p * groups * frames + g * frames
            catalog_ref[0, :, at:at + frames] = found.astype(jnp.bfloat16)
    whole = groups * frames
    catalog_ref[1, :, 0:whole] = catalog_ref[0, :, whole:]
    catalog_ref[1, :, whole:] = -catalog_ref[0, :, 0:whole]
    count = total // groups
    mine = pl.ds(pl.multiple_of(tm * count, count), count)
    scale = 1.0 / whole
    for p in range(2):
        out_ref[:, p, :] = scale * lax.dot_general(
            catalog_ref[p, mine, :], catalog_ref[0], NT, preferred_element_type=jnp.float32
        )


def body(voltages, filter_taps, channel_keep, station_order):
    inputs, frames, n_chan = voltages.shape
    n_taps = filter_taps.shape[0]
    n_sub = channel_keep.shape[0]
    half = station_order.shape[0]
    groups = lax.axis_size("tm")
    stations = lax.axis_size("stn")
    total = stations * inputs
    tile = 2 * inputs
    kept = stations
    weights = pltpu.VMEM((2 * GROUP * n_taps, n_chan), jnp.bfloat16)
    arguments = (voltages, filter_taps, channel_keep.reshape(1, n_sub), station_order.reshape(1, half))
    sums = pl.pallas_call(
        functools.partial(fused_kernel, groups=groups, stations=stations),
        in_specs=[pl.BlockSpec(memory_space=pltpu.HBM)] * 4,
        out_specs=pl.BlockSpec(memory_space=pltpu.VMEM),
        out_shape=jax.ShapeDtypeStruct((total // groups, 2, total), jnp.float32),
        scratch_shapes=[
            pltpu.VMEM((inputs, frames, n_chan), jnp.bfloat16),
            pltpu.VMEM((n_taps, n_chan), jnp.float32),
            pltpu.VMEM((1, n_sub), jnp.int32),
            pltpu.VMEM((1, half), jnp.int32),
            pltpu.VMEM((2 * GROUP * n_taps, inputs * frames), jnp.float32),
            pltpu.VMEM((2, 2 * GROUP, CHUNK), jnp.float32),
            pltpu.VMEM((2 * GROUP, 128), jnp.int32),
            weights,
            weights,
            pltpu.VMEM((GROUP * tile, frames), jnp.float32),
            pltpu.VMEM((kept, tile, frames), jnp.bfloat16),
            pltpu.VMEM((kept, 2, frames), jnp.float32),
            pltpu.VMEM((groups * stations, tile, frames), jnp.bfloat16),
            pltpu.VMEM((groups * stations, 2, frames), jnp.float32),
            pltpu.VMEM((2, total, 2 * groups * frames), jnp.bfloat16),
            pltpu.SemaphoreType.DMA((6,)),
            pltpu.SemaphoreType.DMA((4 + len(CUTS),)),
        ],
        compiler_params=pltpu.CompilerParams(collective_id=0, has_side_effects=True, vmem_limit_bytes=40 << 20),
    )(*[pltpu.with_memory_space_constraint(x, pltpu.HBM) for x in arguments])
    return sums.reshape(total // groups, 1, 2, total)


def solution(mesh):
    placed = (P("stn", "tm", None), P(), P(), P())
    return jax.shard_map(
        body, mesh=mesh, in_specs=placed, out_specs=P("tm", "stn", None, None), check_vma=False
    )
```

```python
import functools
import math

import jax
import jax.numpy as jnp
from jax import lax
from jax.experimental import pallas as pl
from jax.experimental.pallas import tpu as pltpu
from jax.sharding import PartitionSpec as P

SUB_LO = 1024
GROUP = 8
CHUNK = 512
CUTS = (1024, 2048, 3072)
MESH = pl.DeviceIdType.MESH
NT = (((1,), (1,)), ((), ()))


def fused_kernel(
    volt_hbm, taps_hbm, keep_hbm, order_hbm, out_ref, volt_ref, taps_ref, keep_ref, order_ref,
    acc_ref, base_ref, chan_ref, first_ref, later_ref, main_ref, spectra_ref, tails_ref, all_ref, before_ref, catalog_ref,
    sems, load_sems, *, groups, stations,
):
    inputs, frames, n_chan = volt_ref.shape
    n_taps = taps_ref.shape[0]
    n_sub = keep_ref.shape[1]
    unit = 2.0 * math.pi / n_chan
    rows = 2 * GROUP
    turns = stations // GROUP
    span = frames // inputs
    tile = 2 * inputs
    stn = lax.axis_index("stn")
    tm = lax.axis_index("tm")
    devices = groups * stations
    me = stn * groups + tm
    place = tm * stations + stn
    last = groups - 1
    barrier = pltpu.get_barrier_semaphore()
    edges = [0] + [cut for cut in CUTS if cut < n_chan] + [n_chan]
    parts = [slice(lo, hi) for lo, hi in zip(edges[:-1], edges[1:])]

    keep_copy = pltpu.make_async_copy(keep_hbm, keep_ref, load_sems.at[0])
    taps_copy = pltpu.make_async_copy(taps_hbm, taps_ref, load_sems.at[1])
    order_copy = pltpu.make_async_copy(order_hbm, order_ref, load_sems.at[2])
    loads = [
        pltpu.make_async_copy(volt_hbm.at[:, :, part], volt_ref.at[:, :, part], load_sems.at[3 + n])
        for n, part in enumerate(parts)
    ]
    keep_copy.start()
    taps_copy.start()
    for load in loads:
        load.start()
    order_copy.start()

    @pl.loop(1, devices)
    def _(distance):
        device = lax.rem(me + distance, devices)
        pl.semaphore_signal(
            barrier, inc=1, device_id=(device // groups, lax.rem(device, groups)), device_id_type=MESH
        )

    def channels(numbers):
        keep = keep_ref[...]
        before = lax.broadcasted_iota(jnp.int32, (n_sub, n_sub), 0) <= lax.broadcasted_iota(jnp.int32, (n_sub, n_sub), 1)
        count = GROUP * len(numbers)
        keep_rows = jnp.broadcast_to(keep, (count, n_sub))
        rank = jnp.dot(
            keep_rows.astype(jnp.float32).astype(jnp.bfloat16),
            before.astype(jnp.float32).astype(jnp.bfloat16),
            preferred_element_type=jnp.float32,
        )
        slot = jnp.concatenate(
            [lax.broadcasted_iota(jnp.int32, (GROUP, n_sub), 0) + 1 + number * GROUP for number in numbers]
        ).astype(jnp.float32)
        number = lax.broadcasted_iota(jnp.int32, (count, n_sub), 1).astype(jnp.float32)
        hit = jnp.where((rank == slot) & (keep_rows == 1), number, 0.0)
        channel = jnp.sum(hit, axis=1, keepdims=True).astype(jnp.int32) + SUB_LO
        chan_ref[0:count] = jnp.broadcast_to(channel, (count, 128))
        column = lax.broadcasted_iota(jnp.int32, (count, CHUNK), 1)
        angle = ((channel * column) % n_chan).astype(jnp.float32) * unit
        base_ref[0, 0:count] = jnp.cos(angle)
        base_ref[1, 0:count] = jnp.sin(angle)

    def weigh(part, targets):
        count = GROUP * len(targets)
        angle = ((chan_ref[0:count] * (part * CHUNK)) % n_chan).astype(jnp.float32) * unit
        norm = 1.0 / math.sqrt(n_chan)
        cos_step = (jnp.cos(angle) * norm)[:, :1]
        sin_step = (jnp.sin(angle) * norm)[:, :1]
        cos_base = base_ref[0, 0:count]
        sin_base = base_ref[1, 0:count]
        real = cos_step * cos_base - sin_step * sin_base
        imag = -(sin_step * cos_base + cos_step * sin_base)
        columns = pl.ds(part * CHUNK, CHUNK) if isinstance(part, int) else pl.ds(pl.multiple_of(part * CHUNK, CHUNK), CHUNK)
        taps = taps_ref[:, columns]
        for n, w_ref in enumerate(targets):
            own = slice(n * GROUP, (n + 1) * GROUP)
            table = jnp.concatenate([real[own], imag[own]], axis=0).astype(jnp.bfloat16).astype(jnp.float32)
            for tap in range(n_taps):
                w_ref[tap * rows:(tap + 1) * rows, columns] = (table * taps[tap:tap + 1, :]).astype(jnp.bfloat16)

    lane = lax.broadcasted_iota(jnp.int32, (rows, frames), 1)

    def combine(number, product):
        packed = jnp.zeros((rows, frames), jnp.float32)
        for pair in range(inputs // 2):
            sums = product(pair)
            for half in range(2):
                i = 2 * pair + half
                inside = sums[(n_taps - 1) * rows:, half * frames:(half + 1) * frames]
                beyond = jnp.zeros((rows, frames), jnp.float32)
                for tap in range(n_taps - 1):
                    shift = n_taps - 1 - tap
                    piece = pltpu.roll(sums[tap * rows:(tap + 1) * rows, half * frames:(half + 1) * frames], shift, axis=1)
                    beyond = beyond + jnp.where(lane < shift, piece, 0.0)
                    inside = inside + jnp.where(lane < shift, 0.0, piece)
                for p in range(2):
                    main_ref[pl.ds(p * inputs + i, GROUP, stride=tile), :] = inside[p * GROUP:(p + 1) * GROUP]
                packed = packed + (pltpu.roll(beyond, frames - i * span, axis=1) if i > 0 else beyond)
        first = number * GROUP
        spectra_ref[pl.ds(first, GROUP)] = main_ref[...].astype(jnp.bfloat16).reshape(GROUP, tile, frames)
        for p in range(2):
            tails_ref[pl.ds(first, GROUP), p, :] = packed[p * GROUP:(p + 1) * GROUP]

    def send(number):
        first = number * GROUP

        @pl.loop(0, GROUP * groups)
        def _(distance):
            rest = GROUP * groups - groups
            near = jnp.where(distance < groups, distance, groups + lax.rem(me + distance, rest))
            to_stn = first + near // groups
            to_tm = lax.rem(near, groups)

            @pl.when((to_stn != stn) | (to_tm != tm))
            def _():
                pltpu.make_async_remote_copy(
                    src_ref=spectra_ref.at[to_stn],
                    dst_ref=all_ref.at[place],
                    send_sem=sems.at[0],
                    recv_sem=sems.at[1],
                    device_id=(to_stn, to_tm),
                    device_id_type=MESH,
                ).start()

                @pl.when(tm < last)
                def _():
                    pltpu.make_async_remote_copy(
                        src_ref=tails_ref.at[to_stn],
                        dst_ref=before_ref.at[place],
                        send_sem=sems.at[2],
                        recv_sem=sems.at[3],
                        device_id=(to_stn, to_tm),
                        device_id_type=MESH,
                    ).start()

    keep_copy.wait()
    taps_copy.wait()
    channels((0, 1))
    for part in range(n_chan // CHUNK):
        weigh(part, (first_ref, later_ref))

    def partial(part):
        volts = volt_ref[:, :, part].reshape(inputs * frames, part.stop - part.start)
        return lax.dot_general(first_ref[:, part], volts, NT, preferred_element_type=jnp.float32)

    for n, part in enumerate(parts[:-1]):
        loads[n].wait()
        if n == 0:
            acc_ref[...] = partial(part)
        else:
            acc_ref[...] += partial(part)

    loads[-1].wait()

    def first_sums(pair):
        part = parts[-1]
        volts = volt_ref[2 * pair:2 * pair + 2, :, part].reshape(2 * frames, part.stop - part.start)
        found = lax.dot_general(first_ref[:, part], volts, NT, preferred_element_type=jnp.float32)
        return acc_ref[:, 2 * pair * frames:(2 * pair + 2) * frames] + found

    combine(0, first_sums)

    @pl.when(stn > 0)
    def _():
        pl.semaphore_wait(barrier, devices - 1)
        send(0)

    def later_sums(pair):
        volts = volt_ref[2 * pair:2 * pair + 2].reshape(2 * frames, n_chan)
        return lax.dot_general(later_ref[...], volts, NT, preferred_element_type=jnp.float32)

    if turns == 2:
        combine(1, later_sums)

        @pl.when(stn == 0)
        def _():
            pl.semaphore_wait(barrier, devices - 1)
            send(0)

        send(1)
    else:
        @pl.loop(1, turns)
        def _(number):
            @pl.when(number > 1)
            def _():
                channels((number,))

                @pl.loop(0, n_chan // CHUNK)
                def _(part):
                    weigh(part, (later_ref,))

            combine(number, later_sums)

            @pl.when((stn == 0) & (number == 1))
            def _():
                pl.semaphore_wait(barrier, devices - 1)
                send(0)

            send(number)

    own = pltpu.make_async_copy(spectra_ref.at[stn], all_ref.at[place], sems.at[4])
    own.start()

    @pl.when(tm < last)
    def _():
        own_tail = pltpu.make_async_copy(tails_ref.at[stn], before_ref.at[place], sems.at[5])
        own_tail.start()
        own_tail.wait()

    order_copy.wait()
    total = stations * inputs
    half = order_ref.shape[1]
    cols = stations * tile
    row = lax.broadcasted_iota(jnp.int32, (total, half), 0)
    at_station = jnp.where(order_ref[...] == row // 2, 1.0, 0.0).astype(jnp.bfloat16)
    col = lax.broadcasted_iota(jnp.int32, (half, cols), 1)
    station = (col // tile) * (inputs // 2) + (col % inputs) // 2
    spread = jnp.where(station == lax.broadcasted_iota(jnp.int32, (half, cols), 0), 1.0, 0.0).astype(jnp.bfloat16)
    chosen = jnp.dot(at_station, spread, preferred_element_type=jnp.float32)
    row = lax.broadcasted_iota(jnp.int32, (total, cols), 0)
    col = lax.broadcasted_iota(jnp.int32, (total, cols), 1)
    chosen = jnp.where(row % 2 == col % 2, chosen, 0.0)
    side = (col // inputs) % 2
    pick = [jnp.where(side == p, chosen, 0.0).astype(jnp.bfloat16) for p in range(2)]

    own.wait()
    others = all_ref.at[pl.ds(0, devices - 1)]

    def moved(ref, sem):
        return pltpu.make_async_remote_copy(
            src_ref=ref,
            dst_ref=ref,
            send_sem=sems.at[sem],
            recv_sem=sems.at[sem + 1],
            device_id=(stn, lax.rem(tm + 1, groups)),
            device_id_type=MESH,
        )

    moved(others, 0).wait_recv()
    slots = last * stations

    @pl.when(tm < last)
    def _():
        moved(before_ref.at[pl.ds(0, slots - 1)], 2).wait_recv()

    @pl.when(tm == last)
    def _():
        moved(before_ref.at[pl.ds(0, slots)], 2).wait_recv()

    for g in range(groups):
        tiles = all_ref[g * stations:(g + 1) * stations].reshape(cols, frames)
        if g > 0:
            tails = before_ref[(g - 1) * stations:g * stations].reshape(2 * stations, 1, frames)
            tails = jnp.broadcast_to(tails, (2 * stations, inputs, frames)).reshape(cols, frames)
            tails = pltpu.roll(tails, 0, axis=1, stride=span, stride_axis=0)
            early = lax.broadcasted_iota(jnp.int32, (cols, frames), 1) < n_taps - 1
            tiles = (tiles.astype(jnp.float32) + jnp.where(early, tails, 0.0)).astype(jnp.bfloat16)
        for p in range(2):
            found = jnp.dot(pick[p], tiles, preferred_element_type=jnp.float32)
            at = p * groups * frames + g * frames
            catalog_ref[0, :, at:at + frames] = found.astype(jnp.bfloat16)
    whole = groups * frames
    catalog_ref[1, :, 0:whole] = catalog_ref[0, :, whole:]
    catalog_ref[1, :, whole:] = -catalog_ref[0, :, 0:whole]
    count = total // groups
    mine = pl.ds(pl.multiple_of(tm * count, count), count)
    scale = 1.0 / whole
    for p in range(2):
        out_ref[:, p, :] = scale * lax.dot_general(
            catalog_ref[p, mine, :], catalog_ref[0], NT, preferred_element_type=jnp.float32
        )
    moved(others, 0).wait_send()

    @pl.when(tm < last)
    def _():
        moved(before_ref.at[pl.ds(0, devices - 1)], 2).wait_send()


def body(voltages, filter_taps, channel_keep, station_order):
    inputs, frames, n_chan = voltages.shape
    n_taps = filter_taps.shape[0]
    n_sub = channel_keep.shape[0]
    half = station_order.shape[0]
    groups = lax.axis_size("tm")
    stations = lax.axis_size("stn")
    total = stations * inputs
    tile = 2 * inputs
    kept = stations
    weights = pltpu.VMEM((2 * GROUP * n_taps, n_chan), jnp.bfloat16)
    arguments = (voltages, filter_taps, channel_keep.reshape(1, n_sub), station_order.reshape(1, half))
    sums = pl.pallas_call(
        functools.partial(fused_kernel, groups=groups, stations=stations),
        in_specs=[pl.BlockSpec(memory_space=pltpu.HBM)] * 4,
        out_specs=pl.BlockSpec(memory_space=pltpu.VMEM),
        out_shape=jax.ShapeDtypeStruct((total // groups, 2, total), jnp.float32),
        scratch_shapes=[
            pltpu.VMEM((inputs, frames, n_chan), jnp.bfloat16),
            pltpu.VMEM((n_taps, n_chan), jnp.float32),
            pltpu.VMEM((1, n_sub), jnp.int32),
            pltpu.VMEM((1, half), jnp.int32),
            pltpu.VMEM((2 * GROUP * n_taps, inputs * frames), jnp.float32),
            pltpu.VMEM((2, 2 * GROUP, CHUNK), jnp.float32),
            pltpu.VMEM((2 * GROUP, 128), jnp.int32),
            weights,
            weights,
            pltpu.VMEM((GROUP * tile, frames), jnp.float32),
            pltpu.VMEM((kept, tile, frames), jnp.bfloat16),
            pltpu.VMEM((kept, 2, frames), jnp.float32),
            pltpu.VMEM((groups * stations, tile, frames), jnp.bfloat16),
            pltpu.VMEM((groups * stations, 2, frames), jnp.float32),
            pltpu.VMEM((2, total, 2 * groups * frames), jnp.bfloat16),
            pltpu.SemaphoreType.DMA((6,)),
            pltpu.SemaphoreType.DMA((4 + len(CUTS),)),
        ],
        compiler_params=pltpu.CompilerParams(collective_id=0, has_side_effects=True, vmem_limit_bytes=40 << 20),
    )(*[pltpu.with_memory_space_constraint(x, pltpu.HBM) for x in arguments])
    return sums.reshape(total // groups, 1, 2, total)


def solution(mesh):
    placed = (P("stn", "tm", None), P(), P(), P())
    return jax.shard_map(
        body, mesh=mesh, in_specs=placed, out_specs=P("tm", "stn", None, None), check_vma=False
    )
```

```python
import functools
import math

import jax
import jax.numpy as jnp
from jax import lax
from jax.experimental import pallas as pl
from jax.experimental.pallas import tpu as pltpu
from jax.sharding import PartitionSpec as P

SUB_LO = 1024
GROUP = 8
CHUNK = 512
WIDE = 128
CUTS = (1024, 2048, 3072)
MESH = pl.DeviceIdType.MESH
NT = (((1,), (1,)), ((), ()))


def fused_kernel(
    volt_hbm, taps_hbm, keep_hbm, order_hbm, out_ref, volt_ref, taps_ref, keep_ref, order_ref,
    acc_ref, base_ref, first_ref, later_ref, main_ref, spectra_ref, tails_ref, all_ref, before_ref, catalog_ref,
    sems, load_sems, *, groups, stations,
):
    inputs, frames, n_chan = volt_ref.shape
    n_taps = taps_ref.shape[0]
    n_sub = keep_ref.shape[1]
    assert n_chan & (n_chan - 1) == 0 and n_chan <= WIDE * WIDE
    unit = 2.0 * math.pi / n_chan
    rows = 2 * GROUP
    turns = stations // GROUP
    span = frames // inputs
    tile = 2 * inputs
    stn = lax.axis_index("stn")
    tm = lax.axis_index("tm")
    devices = groups * stations
    me = stn * groups + tm
    place = tm * stations + stn
    last = groups - 1
    barrier = pltpu.get_barrier_semaphore()
    edges = [0] + [cut for cut in CUTS if cut < n_chan] + [n_chan]
    parts = [slice(lo, hi) for lo, hi in zip(edges[:-1], edges[1:])]

    keep_copy = pltpu.make_async_copy(keep_hbm, keep_ref, load_sems.at[0])
    taps_copy = pltpu.make_async_copy(taps_hbm, taps_ref, load_sems.at[1])
    order_copy = pltpu.make_async_copy(order_hbm, order_ref, load_sems.at[2])
    loads = [
        pltpu.make_async_copy(volt_hbm.at[:, :, part], volt_ref.at[:, :, part], load_sems.at[3 + n])
        for n, part in enumerate(parts)
    ]
    keep_copy.start()
    taps_copy.start()
    for load in loads:
        load.start()
    order_copy.start()

    @pl.loop(1, devices)
    def _(distance):
        device = lax.rem(me + distance, devices)
        pl.semaphore_signal(
            barrier, inc=1, device_id=(device // groups, lax.rem(device, groups)), device_id_type=MESH
        )

    def channels(numbers):
        keep = keep_ref[...]
        before = lax.broadcasted_iota(jnp.int32, (n_sub, n_sub), 0) <= lax.broadcasted_iota(jnp.int32, (n_sub, n_sub), 1)
        count = GROUP * len(numbers)
        keep_rows = jnp.broadcast_to(keep, (count, n_sub))
        rank = jnp.dot(
            keep_rows.astype(jnp.float32).astype(jnp.bfloat16),
            before.astype(jnp.float32).astype(jnp.bfloat16),
            preferred_element_type=jnp.float32,
        )
        slot = jnp.concatenate(
            [lax.broadcasted_iota(jnp.int32, (GROUP, n_sub), 0) + 1 + number * GROUP for number in numbers]
        ).astype(jnp.float32)
        number = lax.broadcasted_iota(jnp.int32, (count, n_sub), 1).astype(jnp.float32)
        hit = jnp.where((rank == slot) & (keep_rows == 1), number, 0.0)
        channel = jnp.sum(hit, axis=1, keepdims=True).astype(jnp.int32) + SUB_LO
        column = lax.broadcasted_iota(jnp.int32, (count, WIDE), 1)
        norm = 1.0 / math.sqrt(n_chan)
        for n, (pace, size) in enumerate(((1, 1.0), (WIDE, norm))):
            angle = ((channel * (column * pace)) & (n_chan - 1)).astype(jnp.float32) * unit
            base_ref[2 * n, 0:count] = jnp.cos(angle) * size
            base_ref[2 * n + 1, 0:count] = jnp.sin(angle) * size

    def weigh(part, targets):
        count = GROUP * len(targets)
        cos_base, sin_base, cos_all, sin_all = [base_ref[n, 0:count] for n in range(4)]
        real, imag = [], []
        for block in range(CHUNK // WIDE):
            at = part * (CHUNK // WIDE) + block
            cos_step, sin_step = cos_all[:, at:at + 1], sin_all[:, at:at + 1]
            real.append(cos_step * cos_base - sin_step * sin_base)
            imag.append(-(sin_step * cos_base + cos_step * sin_base))
        real, imag = [jnp.concatenate(blocks, axis=1) for blocks in (real, imag)]
        taps = taps_ref[:, part * CHUNK:(part + 1) * CHUNK]
        held = [n for n, piece in enumerate(parts) if piece.start <= part * CHUNK < piece.stop][0]
        columns = slice(part * CHUNK - parts[held].start, (part + 1) * CHUNK - parts[held].start)
        for n, w_refs in enumerate(targets):
            own = slice(n * GROUP, (n + 1) * GROUP)
            table = jnp.concatenate([real[own], imag[own]], axis=0).astype(jnp.bfloat16).astype(jnp.float32)
            for tap in range(n_taps):
                w_refs[held][tap * rows:(tap + 1) * rows, columns] = (table * taps[tap:tap + 1, :]).astype(jnp.bfloat16)

    lane = lax.broadcasted_iota(jnp.int32, (rows, frames), 1)

    def combine(number, product):
        packed = jnp.zeros((rows, frames), jnp.float32)
        for pair in range(inputs // 2):
            sums = product(pair)
            for half in range(2):
                i = 2 * pair + half
                inside = sums[(n_taps - 1) * rows:, half * frames:(half + 1) * frames]
                beyond = jnp.zeros((rows, frames), jnp.float32)
                for tap in range(n_taps - 1):
                    shift = n_taps - 1 - tap
                    piece = pltpu.roll(sums[tap * rows:(tap + 1) * rows, half * frames:(half + 1) * frames], shift, axis=1)
                    beyond = beyond + jnp.where(lane < shift, piece, 0.0)
                    inside = inside + jnp.where(lane < shift, 0.0, piece)
                for p in range(2):
                    main_ref[pl.ds(p * inputs + i, GROUP, stride=tile), :] = inside[p * GROUP:(p + 1) * GROUP]
                packed = packed + (pltpu.roll(beyond, frames - i * span, axis=1) if i > 0 else beyond)
        first = number * GROUP
        spectra_ref[pl.ds(first, GROUP)] = main_ref[...].astype(jnp.bfloat16).reshape(GROUP, tile, frames)
        for p in range(2):
            tails_ref[pl.ds(first, GROUP), p, :] = packed[p * GROUP:(p + 1) * GROUP]

    def send(number):
        first = number * GROUP

        @pl.loop(0, GROUP * groups)
        def _(distance):
            rest = GROUP * groups - groups
            near = jnp.where(distance < groups, distance, groups + lax.rem(me + distance, rest))
            to_stn = first + near // groups
            to_tm = lax.rem(near, groups)

            @pl.when((to_stn != stn) | (to_tm != tm))
            def _():
                pltpu.make_async_remote_copy(
                    src_ref=spectra_ref.at[to_stn],
                    dst_ref=all_ref.at[place],
                    send_sem=sems.at[0],
                    recv_sem=sems.at[1],
                    device_id=(to_stn, to_tm),
                    device_id_type=MESH,
                ).start()

                @pl.when(tm < last)
                def _():
                    pltpu.make_async_remote_copy(
                        src_ref=tails_ref.at[to_stn],
                        dst_ref=before_ref.at[place],
                        send_sem=sems.at[2],
                        recv_sem=sems.at[3],
                        device_id=(to_stn, to_tm),
                        device_id_type=MESH,
                    ).start()

    keep_copy.wait()
    taps_copy.wait()
    channels((0, 1))
    def weigh_piece(n, targets):
        for part in range(parts[n].start // CHUNK, parts[n].stop // CHUNK):
            weigh(part, targets)

    weigh_piece(0, (first_ref, later_ref))

    def partial(n, pair, w_refs):
        volts = volt_ref[2 * pair:2 * pair + 2, :, parts[n]].reshape(2 * frames, parts[n].stop - parts[n].start)
        return lax.dot_general(w_refs[n][...], volts, NT, preferred_element_type=jnp.float32)

    for n in range(len(parts) - 1):
        loads[n].wait()
        for pair in range(inputs // 2):
            found = partial(n, pair, first_ref)
            at = slice(2 * pair * frames, (2 * pair + 2) * frames)
            acc_ref[:, at] = found if n == 0 else acc_ref[:, at] + found
        weigh_piece(n + 1, (first_ref, later_ref))

    loads[-1].wait()

    def first_sums(pair):
        return acc_ref[:, 2 * pair * frames:(2 * pair + 2) * frames] + partial(len(parts) - 1, pair, first_ref)

    combine(0, first_sums)

    @pl.when(stn > 0)
    def _():
        pl.semaphore_wait(barrier, devices - 1)
        send(0)

    def later_sums(pair):
        return sum(partial(n, pair, later_ref) for n in range(len(parts)))

    if turns == 2:
        combine(1, later_sums)

        @pl.when(stn == 0)
        def _():
            pl.semaphore_wait(barrier, devices - 1)
            send(0)

        send(1)
    else:
        @pl.loop(1, turns)
        def _(number):
            @pl.when(number > 1)
            def _():
                channels((number,))

                for n in range(len(parts)):
                    weigh_piece(n, (later_ref,))

            combine(number, later_sums)

            @pl.when((stn == 0) & (number == 1))
            def _():
                pl.semaphore_wait(barrier, devices - 1)
                send(0)

            send(number)

    own = pltpu.make_async_copy(spectra_ref.at[stn], all_ref.at[place], sems.at[4])
    own.start()

    @pl.when(tm < last)
    def _():
        own_tail = pltpu.make_async_copy(tails_ref.at[stn], before_ref.at[place], sems.at[5])
        own_tail.start()
        own_tail.wait()

    order_copy.wait()
    total = stations * inputs
    half = order_ref.shape[1]
    cols = stations * tile
    row = lax.broadcasted_iota(jnp.int32, (total, half), 0)
    at_station = jnp.where(order_ref[...] == row // 2, 1.0, 0.0).astype(jnp.bfloat16)
    col = lax.broadcasted_iota(jnp.int32, (half, cols), 1)
    station = (col // tile) * (inputs // 2) + (col % inputs) // 2
    spread = jnp.where(station == lax.broadcasted_iota(jnp.int32, (half, cols), 0), 1.0, 0.0).astype(jnp.bfloat16)
    chosen = jnp.dot(at_station, spread, preferred_element_type=jnp.float32)
    row = lax.broadcasted_iota(jnp.int32, (total, cols), 0)
    col = lax.broadcasted_iota(jnp.int32, (total, cols), 1)
    chosen = jnp.where(row % 2 == col % 2, chosen, 0.0)
    side = (col // inputs) % 2
    pick = [jnp.where(side == p, chosen, 0.0).astype(jnp.bfloat16) for p in range(2)]

    own.wait()
    others = all_ref.at[pl.ds(0, devices - 1)]

    def moved(ref, sem):
        return pltpu.make_async_remote_copy(
            src_ref=ref,
            dst_ref=ref,
            send_sem=sems.at[sem],
            recv_sem=sems.at[sem + 1],
            device_id=(stn, lax.rem(tm + 1, groups)),
            device_id_type=MESH,
        )

    moved(others, 0).wait_recv()
    slots = last * stations

    @pl.when(tm < last)
    def _():
        moved(before_ref.at[pl.ds(0, slots - 1)], 2).wait_recv()

    @pl.when(tm == last)
    def _():
        moved(before_ref.at[pl.ds(0, slots)], 2).wait_recv()

    for g in range(groups):
        tiles = all_ref[g * stations:(g + 1) * stations].reshape(cols, frames)
        if g > 0:
            tails = before_ref[(g - 1) * stations:g * stations].reshape(2 * stations, 1, frames)
            tails = jnp.broadcast_to(tails, (2 * stations, inputs, frames)).reshape(cols, frames)
            tails = pltpu.roll(tails, 0, axis=1, stride=span, stride_axis=0)
            early = lax.broadcasted_iota(jnp.int32, (cols, frames), 1) < n_taps - 1
            tiles = (tiles.astype(jnp.float32) + jnp.where(early, tails, 0.0)).astype(jnp.bfloat16)
        for p in range(2):
            found = jnp.dot(pick[p], tiles, preferred_element_type=jnp.float32)
            at = p * groups * frames + g * frames
            catalog_ref[0, :, at:at + frames] = found.astype(jnp.bfloat16)
    whole = groups * frames
    catalog_ref[1, :, 0:whole] = catalog_ref[0, :, whole:]
    catalog_ref[1, :, whole:] = -catalog_ref[0, :, 0:whole]
    count = total // groups
    mine = pl.ds(pl.multiple_of(tm * count, count), count)
    scale = 1.0 / whole
    for p in range(2):
        out_ref[:, p, :] = scale * lax.dot_general(
            catalog_ref[p, mine, :], catalog_ref[0], NT, preferred_element_type=jnp.float32
        )
    moved(others, 0).wait_send()

    @pl.when(tm < last)
    def _():
        moved(before_ref.at[pl.ds(0, devices - 1)], 2).wait_send()


def body(voltages, filter_taps, channel_keep, station_order):
    inputs, frames, n_chan = voltages.shape
    n_taps = filter_taps.shape[0]
    n_sub = channel_keep.shape[0]
    half = station_order.shape[0]
    groups = lax.axis_size("tm")
    stations = lax.axis_size("stn")
    total = stations * inputs
    tile = 2 * inputs
    kept = stations
    edges = [0] + [cut for cut in CUTS if cut < n_chan] + [n_chan]
    weights = tuple(
        pltpu.VMEM((2 * GROUP * n_taps, hi - lo), jnp.bfloat16) for lo, hi in zip(edges[:-1], edges[1:])
    )
    arguments = (voltages, filter_taps, channel_keep.reshape(1, n_sub), station_order.reshape(1, half))
    sums = pl.pallas_call(
        functools.partial(fused_kernel, groups=groups, stations=stations),
        in_specs=[pl.BlockSpec(memory_space=pltpu.HBM)] * 4,
        out_specs=pl.BlockSpec(memory_space=pltpu.VMEM),
        out_shape=jax.ShapeDtypeStruct((total // groups, 2, total), jnp.float32),
        scratch_shapes=[
            pltpu.VMEM((inputs, frames, n_chan), jnp.bfloat16),
            pltpu.VMEM((n_taps, n_chan), jnp.float32),
            pltpu.VMEM((1, n_sub), jnp.int32),
            pltpu.VMEM((1, half), jnp.int32),
            pltpu.VMEM((2 * GROUP * n_taps, inputs * frames), jnp.float32),
            pltpu.VMEM((4, 2 * GROUP, WIDE), jnp.float32),
            weights,
            weights,
            pltpu.VMEM((GROUP * tile, frames), jnp.float32),
            pltpu.VMEM((kept, tile, frames), jnp.bfloat16),
            pltpu.VMEM((kept, 2, frames), jnp.float32),
            pltpu.VMEM((groups * stations, tile, frames), jnp.bfloat16),
            pltpu.VMEM((groups * stations, 2, frames), jnp.float32),
            pltpu.VMEM((2, total, 2 * groups * frames), jnp.bfloat16),
            pltpu.SemaphoreType.DMA((6,)),
            pltpu.SemaphoreType.DMA((4 + len(CUTS),)),
        ],
        compiler_params=pltpu.CompilerParams(collective_id=0, has_side_effects=True, vmem_limit_bytes=40 << 20),
    )(*[pltpu.with_memory_space_constraint(x, pltpu.HBM) for x in arguments])
    return sums.reshape(total // groups, 1, 2, total)


def solution(mesh):
    placed = (P("stn", "tm", None), P(), P(), P())
    return jax.shard_map(
        body, mesh=mesh, in_specs=placed, out_specs=P("tm", "stn", None, None), check_vma=False
    )
```

```python
import functools
import math

import jax
import jax.numpy as jnp
from jax import lax
from jax.experimental import pallas as pl
from jax.experimental.pallas import tpu as pltpu
from jax.sharding import PartitionSpec as P

SUB_LO = 1024
GROUP = 8
CHUNK = 512
WIDE = 128
ORDER = ((0, 1, 2, 4, 3, 5, 6, 7), (0, 1, 4, 2, 5, 6, 3, 7))
CUTS = (1024, 2048, 3072)
MESH = pl.DeviceIdType.MESH
NT = (((1,), (1,)), ((), ()))


def fused_kernel(
    volt_hbm, taps_hbm, keep_hbm, order_hbm, out_ref, volt_ref, taps_ref, keep_ref, order_ref,
    acc_ref, base_ref, first_ref, later_ref, main_ref, spectra_ref, tails_ref, all_ref, before_ref, catalog_ref,
    sems, load_sems, *, groups, stations,
):
    inputs, frames, n_chan = volt_ref.shape
    n_taps = taps_ref.shape[0]
    n_sub = keep_ref.shape[1]
    assert n_chan & (n_chan - 1) == 0 and n_chan <= WIDE * WIDE
    unit = 2.0 * math.pi / n_chan
    rows = 2 * GROUP
    turns = stations // GROUP
    span = frames // inputs
    tile = 2 * inputs
    stn = lax.axis_index("stn")
    tm = lax.axis_index("tm")
    devices = groups * stations
    me = stn * groups + tm
    place = tm * stations + stn
    last = groups - 1
    barrier = pltpu.get_barrier_semaphore()
    edges = [0] + [cut for cut in CUTS if cut < n_chan] + [n_chan]
    parts = [slice(lo, hi) for lo, hi in zip(edges[:-1], edges[1:])]

    keep_copy = pltpu.make_async_copy(keep_hbm, keep_ref, load_sems.at[0])
    taps_copy = pltpu.make_async_copy(taps_hbm, taps_ref, load_sems.at[1])
    order_copy = pltpu.make_async_copy(order_hbm, order_ref, load_sems.at[2])
    loads = [
        pltpu.make_async_copy(volt_hbm.at[:, :, part], volt_ref.at[:, :, part], load_sems.at[3 + n])
        for n, part in enumerate(parts)
    ]
    keep_copy.start()
    taps_copy.start()
    for load in loads:
        load.start()
    order_copy.start()

    @pl.loop(1, devices)
    def _(distance):
        device = lax.rem(me + distance, devices)
        pl.semaphore_signal(
            barrier, inc=1, device_id=(device // groups, lax.rem(device, groups)), device_id_type=MESH
        )

    def channels(numbers):
        keep = keep_ref[...]
        before = lax.broadcasted_iota(jnp.int32, (n_sub, n_sub), 0) <= lax.broadcasted_iota(jnp.int32, (n_sub, n_sub), 1)
        count = GROUP * len(numbers)
        keep_rows = jnp.broadcast_to(keep, (count, n_sub))
        rank = jnp.dot(
            keep_rows.astype(jnp.float32).astype(jnp.bfloat16),
            before.astype(jnp.float32).astype(jnp.bfloat16),
            preferred_element_type=jnp.float32,
        )
        slot = jnp.concatenate(
            [lax.broadcasted_iota(jnp.int32, (GROUP, n_sub), 0) + 1 + number * GROUP for number in numbers]
        ).astype(jnp.float32)
        number = lax.broadcasted_iota(jnp.int32, (count, n_sub), 1).astype(jnp.float32)
        hit = jnp.where((rank == slot) & (keep_rows == 1), number, 0.0)
        channel = jnp.sum(hit, axis=1, keepdims=True).astype(jnp.int32) + SUB_LO
        column = lax.broadcasted_iota(jnp.int32, (count, WIDE), 1)
        norm = 1.0 / math.sqrt(n_chan)
        for n, (pace, size) in enumerate(((1, 1.0), (WIDE, norm))):
            angle = ((channel * (column * pace)) & (n_chan - 1)).astype(jnp.float32) * unit
            base_ref[2 * n, 0:count] = jnp.cos(angle) * size
            base_ref[2 * n + 1, 0:count] = jnp.sin(angle) * size

    def weigh(part, targets):
        count = GROUP * len(targets)
        cos_base, sin_base, cos_all, sin_all = [base_ref[n, 0:count] for n in range(4)]
        real, imag = [], []
        for block in range(CHUNK // WIDE):
            at = part * (CHUNK // WIDE) + block
            cos_step, sin_step = cos_all[:, at:at + 1], sin_all[:, at:at + 1]
            real.append(cos_step * cos_base - sin_step * sin_base)
            imag.append(-(sin_step * cos_base + cos_step * sin_base))
        real, imag = [jnp.concatenate(blocks, axis=1) for blocks in (real, imag)]
        taps = taps_ref[:, part * CHUNK:(part + 1) * CHUNK]
        held = [n for n, piece in enumerate(parts) if piece.start <= part * CHUNK < piece.stop][0]
        columns = slice(part * CHUNK - parts[held].start, (part + 1) * CHUNK - parts[held].start)
        for n, w_refs in enumerate(targets):
            own = slice(n * GROUP, (n + 1) * GROUP)
            table = jnp.concatenate([real[own], imag[own]], axis=0).astype(jnp.bfloat16).astype(jnp.float32)
            for tap in range(n_taps):
                w_refs[held][tap * rows:(tap + 1) * rows, columns] = (table * taps[tap:tap + 1, :]).astype(jnp.bfloat16)

    lane = lax.broadcasted_iota(jnp.int32, (rows, frames), 1)

    def combine(number, product):
        packed = jnp.zeros((rows, frames), jnp.float32)
        for pair in range(inputs // 2):
            sums = product(pair)
            for half in range(2):
                i = 2 * pair + half
                inside = sums[(n_taps - 1) * rows:, half * frames:(half + 1) * frames]
                beyond = jnp.zeros((rows, frames), jnp.float32)
                for tap in range(n_taps - 1):
                    shift = n_taps - 1 - tap
                    piece = pltpu.roll(sums[tap * rows:(tap + 1) * rows, half * frames:(half + 1) * frames], shift, axis=1)
                    beyond = beyond + jnp.where(lane < shift, piece, 0.0)
                    inside = inside + jnp.where(lane < shift, 0.0, piece)
                for p in range(2):
                    main_ref[pl.ds(p * inputs + i, GROUP, stride=tile), :] = inside[p * GROUP:(p + 1) * GROUP]
                packed = packed + (pltpu.roll(beyond, frames - i * span, axis=1) if i > 0 else beyond)
        first = number * GROUP
        spectra_ref[pl.ds(first, GROUP)] = main_ref[...].astype(jnp.bfloat16).reshape(GROUP, tile, frames)
        for p in range(2):
            tails_ref[pl.ds(first, GROUP), p, :] = packed[p * GROUP:(p + 1) * GROUP]

    def send(number):
        first = number * GROUP

        def to(to_stn, to_tm):
            @pl.when((to_stn != stn) | (to_tm != tm))
            def _():
                pltpu.make_async_remote_copy(
                    src_ref=spectra_ref.at[to_stn],
                    dst_ref=all_ref.at[place],
                    send_sem=sems.at[0],
                    recv_sem=sems.at[1],
                    device_id=(to_stn, to_tm),
                    device_id_type=MESH,
                ).start()

                @pl.when(tm < last)
                def _():
                    pltpu.make_async_remote_copy(
                        src_ref=tails_ref.at[to_stn],
                        dst_ref=before_ref.at[place],
                        send_sem=sems.at[2],
                        recv_sem=sems.at[3],
                        device_id=(to_stn, to_tm),
                        device_id_type=MESH,
                    ).start()

        for chip in ORDER[0 if isinstance(number, int) and number == 0 else 1]:
            for core in range(groups):
                to(first + chip, core)

    keep_copy.wait()
    taps_copy.wait()
    channels((0, 1))
    def weigh_piece(n, targets):
        for part in range(parts[n].start // CHUNK, parts[n].stop // CHUNK):
            weigh(part, targets)

    weigh_piece(0, (first_ref, later_ref))

    def partial(n, pair, w_refs):
        volts = volt_ref[2 * pair:2 * pair + 2, :, parts[n]].reshape(2 * frames, parts[n].stop - parts[n].start)
        return lax.dot_general(w_refs[n][...], volts, NT, preferred_element_type=jnp.float32)

    for n in range(len(parts) - 1):
        loads[n].wait()
        for pair in range(inputs // 2):
            found = partial(n, pair, first_ref)
            at = slice(2 * pair * frames, (2 * pair + 2) * frames)
            acc_ref[:, at] = found if n == 0 else acc_ref[:, at] + found
        weigh_piece(n + 1, (first_ref, later_ref))

    loads[-1].wait()

    def first_sums(pair):
        return acc_ref[:, 2 * pair * frames:(2 * pair + 2) * frames] + partial(len(parts) - 1, pair, first_ref)

    combine(0, first_sums)

    @pl.when(stn > 0)
    def _():
        pl.semaphore_wait(barrier, devices - 1)
        send(0)

    def later_sums(pair):
        return sum(partial(n, pair, later_ref) for n in range(len(parts)))

    if turns == 2:
        combine(1, later_sums)

        @pl.when(stn == 0)
        def _():
            pl.semaphore_wait(barrier, devices - 1)
            send(0)

        send(1)
    else:
        @pl.loop(1, turns)
        def _(number):
            @pl.when(number > 1)
            def _():
                channels((number,))

                for n in range(len(parts)):
                    weigh_piece(n, (later_ref,))

            combine(number, later_sums)

            @pl.when((stn == 0) & (number == 1))
            def _():
                pl.semaphore_wait(barrier, devices - 1)
                send(0)

            send(number)

    own = pltpu.make_async_copy(spectra_ref.at[stn], all_ref.at[place], sems.at[4])
    own.start()

    @pl.when(tm < last)
    def _():
        own_tail = pltpu.make_async_copy(tails_ref.at[stn], before_ref.at[place], sems.at[5])
        own_tail.start()
        own_tail.wait()

    order_copy.wait()
    total = stations * inputs
    half = order_ref.shape[1]
    cols = stations * tile
    row = lax.broadcasted_iota(jnp.int32, (total, half), 0)
    at_station = jnp.where(order_ref[...] == row // 2, 1.0, 0.0).astype(jnp.bfloat16)
    col = lax.broadcasted_iota(jnp.int32, (half, cols), 1)
    station = (col // tile) * (inputs // 2) + (col % inputs) // 2
    spread = jnp.where(station == lax.broadcasted_iota(jnp.int32, (half, cols), 0), 1.0, 0.0).astype(jnp.bfloat16)
    chosen = jnp.dot(at_station, spread, preferred_element_type=jnp.float32)
    row = lax.broadcasted_iota(jnp.int32, (total, cols), 0)
    col = lax.broadcasted_iota(jnp.int32, (total, cols), 1)
    chosen = jnp.where(row % 2 == col % 2, chosen, 0.0)
    side = (col // inputs) % 2
    pick = [jnp.where(side == p, chosen, 0.0).astype(jnp.bfloat16) for p in range(2)]

    own.wait()
    others = all_ref.at[pl.ds(0, devices - 1)]

    def moved(ref, sem):
        return pltpu.make_async_remote_copy(
            src_ref=ref,
            dst_ref=ref,
            send_sem=sems.at[sem],
            recv_sem=sems.at[sem + 1],
            device_id=(stn, lax.rem(tm + 1, groups)),
            device_id_type=MESH,
        )

    moved(others, 0).wait_recv()
    slots = last * stations

    @pl.when(tm < last)
    def _():
        moved(before_ref.at[pl.ds(0, slots - 1)], 2).wait_recv()

    @pl.when(tm == last)
    def _():
        moved(before_ref.at[pl.ds(0, slots)], 2).wait_recv()

    for g in range(groups):
        tiles = all_ref[g * stations:(g + 1) * stations].reshape(cols, frames)
        if g > 0:
            tails = before_ref[(g - 1) * stations:g * stations].reshape(2 * stations, 1, frames)
            tails = jnp.broadcast_to(tails, (2 * stations, inputs, frames)).reshape(cols, frames)
            tails = pltpu.roll(tails, 0, axis=1, stride=span, stride_axis=0)
            early = lax.broadcasted_iota(jnp.int32, (cols, frames), 1) < n_taps - 1
            tiles = (tiles.astype(jnp.float32) + jnp.where(early, tails, 0.0)).astype(jnp.bfloat16)
        for p in range(2):
            found = jnp.dot(pick[p], tiles, preferred_element_type=jnp.float32)
            at = p * groups * frames + g * frames
            catalog_ref[0, :, at:at + frames] = found.astype(jnp.bfloat16)
    whole = groups * frames
    catalog_ref[1, :, 0:whole] = catalog_ref[0, :, whole:]
    catalog_ref[1, :, whole:] = -catalog_ref[0, :, 0:whole]
    count = total // groups
    mine = pl.ds(pl.multiple_of(tm * count, count), count)
    scale = 1.0 / whole
    for p in range(2):
        out_ref[:, p, :] = scale * lax.dot_general(
            catalog_ref[p, mine, :], catalog_ref[0], NT, preferred_element_type=jnp.float32
        )
    moved(others, 0).wait_send()

    @pl.when(tm < last)
    def _():
        moved(before_ref.at[pl.ds(0, devices - 1)], 2).wait_send()


def body(voltages, filter_taps, channel_keep, station_order):
    inputs, frames, n_chan = voltages.shape
    n_taps = filter_taps.shape[0]
    n_sub = channel_keep.shape[0]
    half = station_order.shape[0]
    groups = lax.axis_size("tm")
    stations = lax.axis_size("stn")
    total = stations * inputs
    tile = 2 * inputs
    kept = stations
    edges = [0] + [cut for cut in CUTS if cut < n_chan] + [n_chan]
    weights = tuple(
        pltpu.VMEM((2 * GROUP * n_taps, hi - lo), jnp.bfloat16) for lo, hi in zip(edges[:-1], edges[1:])
    )
    arguments = (voltages, filter_taps, channel_keep.reshape(1, n_sub), station_order.reshape(1, half))
    sums = pl.pallas_call(
        functools.partial(fused_kernel, groups=groups, stations=stations),
        in_specs=[pl.BlockSpec(memory_space=pltpu.HBM)] * 4,
        out_specs=pl.BlockSpec(memory_space=pltpu.VMEM),
        out_shape=jax.ShapeDtypeStruct((total // groups, 2, total), jnp.float32),
        scratch_shapes=[
            pltpu.VMEM((inputs, frames, n_chan), jnp.bfloat16),
            pltpu.VMEM((n_taps, n_chan), jnp.float32),
            pltpu.VMEM((1, n_sub), jnp.int32),
            pltpu.VMEM((1, half), jnp.int32),
            pltpu.VMEM((2 * GROUP * n_taps, inputs * frames), jnp.float32),
            pltpu.VMEM((4, 2 * GROUP, WIDE), jnp.float32),
            weights,
            weights,
            pltpu.VMEM((GROUP * tile, frames), jnp.float32),
            pltpu.VMEM((kept, tile, frames), jnp.bfloat16),
            pltpu.VMEM((kept, 2, frames), jnp.float32),
            pltpu.VMEM((groups * stations, tile, frames), jnp.bfloat16),
            pltpu.VMEM((groups * stations, 2, frames), jnp.float32),
            pltpu.VMEM((2, total, 2 * groups * frames), jnp.bfloat16),
            pltpu.SemaphoreType.DMA((6,)),
            pltpu.SemaphoreType.DMA((4 + len(CUTS),)),
        ],
        compiler_params=pltpu.CompilerParams(collective_id=0, has_side_effects=True, vmem_limit_bytes=40 << 20),
    )(*[pltpu.with_memory_space_constraint(x, pltpu.HBM) for x in arguments])
    return sums.reshape(total // groups, 1, 2, total)


def solution(mesh):
    placed = (P("stn", "tm", None), P(), P(), P())
    return jax.shard_map(
        body, mesh=mesh, in_specs=placed, out_specs=P("tm", "stn", None, None), check_vma=False
    )
```

```python
import functools
import math

import jax
import jax.numpy as jnp
from jax import lax
from jax.experimental import pallas as pl
from jax.experimental.pallas import tpu as pltpu
from jax.sharding import PartitionSpec as P

SUB_LO = 1024
GROUP = 8
CHUNK = 512
WIDE = 128
ORDER = ((0, 1, 2, 4, 3, 5, 6, 7), (0, 1, 4, 2, 5, 6, 3, 7))
CUTS = (1024, 2048, 3072)
MESH = pl.DeviceIdType.MESH
NT = (((1,), (1,)), ((), ()))


def fused_kernel(
    volt_hbm, taps_hbm, keep_hbm, order_hbm, out_ref, volt_ref, taps_ref, keep_ref, order_ref,
    acc_ref, base_ref, first_ref, later_ref, main_ref, spectra_ref, tails_ref, all_ref, before_ref, catalog_ref,
    sems, load_sems, *, groups, stations,
):
    inputs, frames, n_chan = volt_ref.shape
    n_taps = taps_ref.shape[0]
    n_sub = keep_ref.shape[1]
    assert n_chan & (n_chan - 1) == 0 and n_chan <= WIDE * WIDE
    unit = 2.0 * math.pi / n_chan
    rows = 2 * GROUP
    turns = stations // GROUP
    span = frames // inputs
    tile = 2 * inputs
    stn = lax.axis_index("stn")
    tm = lax.axis_index("tm")
    devices = groups * stations
    me = stn * groups + tm
    place = tm * stations + stn
    last = groups - 1
    barrier = pltpu.get_barrier_semaphore()
    edges = [0] + [cut for cut in CUTS if cut < n_chan] + [n_chan]
    parts = [slice(lo, hi) for lo, hi in zip(edges[:-1], edges[1:])]

    keep_copy = pltpu.make_async_copy(keep_hbm, keep_ref, load_sems.at[0])
    taps_copy = pltpu.make_async_copy(taps_hbm, taps_ref, load_sems.at[1])
    order_copy = pltpu.make_async_copy(order_hbm, order_ref, load_sems.at[2])
    loads = [
        pltpu.make_async_copy(volt_hbm.at[:, :, part], volt_ref.at[:, :, part], load_sems.at[3 + n])
        for n, part in enumerate(parts)
    ]
    keep_copy.start()
    taps_copy.start()
    for load in loads:
        load.start()
    order_copy.start()

    @pl.loop(1, devices)
    def _(distance):
        device = lax.rem(me + distance, devices)
        pl.semaphore_signal(
            barrier, inc=1, device_id=(device // groups, lax.rem(device, groups)), device_id_type=MESH
        )

    def channels(numbers):
        keep = keep_ref[...]
        before = lax.broadcasted_iota(jnp.int32, (n_sub, n_sub), 0) <= lax.broadcasted_iota(jnp.int32, (n_sub, n_sub), 1)
        count = GROUP * len(numbers)
        keep_rows = jnp.broadcast_to(keep, (count, n_sub))
        rank = jnp.dot(
            keep_rows.astype(jnp.float32).astype(jnp.bfloat16),
            before.astype(jnp.float32).astype(jnp.bfloat16),
            preferred_element_type=jnp.float32,
        )
        slot = jnp.concatenate(
            [lax.broadcasted_iota(jnp.int32, (GROUP, n_sub), 0) + 1 + number * GROUP for number in numbers]
        ).astype(jnp.float32)
        number = lax.broadcasted_iota(jnp.int32, (count, n_sub), 1).astype(jnp.float32)
        hit = jnp.where((rank == slot) & (keep_rows == 1), number, 0.0)
        channel = jnp.sum(hit, axis=1, keepdims=True).astype(jnp.int32) + SUB_LO
        column = lax.broadcasted_iota(jnp.int32, (count, WIDE), 1)
        norm = 1.0 / math.sqrt(n_chan)
        for n, (pace, size) in enumerate(((1, 1.0), (WIDE, norm))):
            angle = ((channel * (column * pace)) & (n_chan - 1)).astype(jnp.float32) * unit
            base_ref[2 * n, 0:count] = jnp.cos(angle) * size
            base_ref[2 * n + 1, 0:count] = jnp.sin(angle) * size

    def weigh(part, targets, skip=0):
        count = GROUP * len(targets)
        lines = slice(skip * GROUP, skip * GROUP + count)
        cos_base, sin_base, cos_all, sin_all = [base_ref[n, lines] for n in range(4)]
        real, imag = [], []
        for block in range(CHUNK // WIDE):
            at = part * (CHUNK // WIDE) + block
            cos_step, sin_step = cos_all[:, at:at + 1], sin_all[:, at:at + 1]
            real.append(cos_step * cos_base - sin_step * sin_base)
            imag.append(-(sin_step * cos_base + cos_step * sin_base))
        real, imag = [jnp.concatenate(blocks, axis=1) for blocks in (real, imag)]
        taps = taps_ref[:, part * CHUNK:(part + 1) * CHUNK]
        held = [n for n, piece in enumerate(parts) if piece.start <= part * CHUNK < piece.stop][0]
        columns = slice(part * CHUNK - parts[held].start, (part + 1) * CHUNK - parts[held].start)
        for n, w_refs in enumerate(targets):
            own = slice(n * GROUP, (n + 1) * GROUP)
            table = jnp.concatenate([real[own], imag[own]], axis=0).astype(jnp.bfloat16).astype(jnp.float32)
            for tap in range(n_taps):
                w_refs[held][tap * rows:(tap + 1) * rows, columns] = (table * taps[tap:tap + 1, :]).astype(jnp.bfloat16)

    lane = lax.broadcasted_iota(jnp.int32, (rows, frames), 1)

    def combine(number, product):
        packed = jnp.zeros((rows, frames), jnp.float32)
        for pair in range(inputs // 2):
            sums = product(pair)
            for half in range(2):
                i = 2 * pair + half
                inside = sums[(n_taps - 1) * rows:, half * frames:(half + 1) * frames]
                beyond = jnp.zeros((rows, frames), jnp.float32)
                for tap in range(n_taps - 1):
                    shift = n_taps - 1 - tap
                    piece = pltpu.roll(sums[tap * rows:(tap + 1) * rows, half * frames:(half + 1) * frames], shift, axis=1)
                    beyond = beyond + jnp.where(lane < shift, piece, 0.0)
                    inside = inside + jnp.where(lane < shift, 0.0, piece)
                for p in range(2):
                    main_ref[pl.ds(p * inputs + i, GROUP, stride=tile), :] = inside[p * GROUP:(p + 1) * GROUP]
                packed = packed + (pltpu.roll(beyond, frames - i * span, axis=1) if i > 0 else beyond)
        first = number * GROUP
        spectra_ref[pl.ds(first, GROUP)] = main_ref[...].astype(jnp.bfloat16).reshape(GROUP, tile, frames)
        for p in range(2):
            tails_ref[pl.ds(first, GROUP), p, :] = packed[p * GROUP:(p + 1) * GROUP]

    def send(number):
        first = number * GROUP

        def to(to_stn, to_tm):
            @pl.when((to_stn != stn) | (to_tm != tm))
            def _():
                pltpu.make_async_remote_copy(
                    src_ref=spectra_ref.at[to_stn],
                    dst_ref=all_ref.at[place],
                    send_sem=sems.at[0],
                    recv_sem=sems.at[1],
                    device_id=(to_stn, to_tm),
                    device_id_type=MESH,
                ).start()

                @pl.when(tm < last)
                def _():
                    pltpu.make_async_remote_copy(
                        src_ref=tails_ref.at[to_stn],
                        dst_ref=before_ref.at[place],
                        send_sem=sems.at[2],
                        recv_sem=sems.at[3],
                        device_id=(to_stn, to_tm),
                        device_id_type=MESH,
                    ).start()

        for chip in ORDER[0 if isinstance(number, int) and number == 0 else 1]:
            for core in range(groups):
                to(first + chip, core)

    keep_copy.wait()
    taps_copy.wait()
    channels((0, 1))
    def weigh_piece(n, targets, skip=0):
        for part in range(parts[n].start // CHUNK, parts[n].stop // CHUNK):
            weigh(part, targets, skip)

    for n in range(len(parts)):
        weigh_piece(n, (first_ref,), 0)

    def partial(n, pair, w_refs):
        volts = volt_ref[2 * pair:2 * pair + 2, :, parts[n]].reshape(2 * frames, parts[n].stop - parts[n].start)
        return lax.dot_general(w_refs[n][...], volts, NT, preferred_element_type=jnp.float32)

    for n in range(len(parts) - 1):
        loads[n].wait()
        for pair in range(inputs // 2):
            found = partial(n, pair, first_ref)
            at = slice(2 * pair * frames, (2 * pair + 2) * frames)
            acc_ref[:, at] = found if n == 0 else acc_ref[:, at] + found

    loads[-1].wait()

    def first_sums(pair):
        return acc_ref[:, 2 * pair * frames:(2 * pair + 2) * frames] + partial(len(parts) - 1, pair, first_ref)

    combine(0, first_sums)

    @pl.when(stn > 0)
    def _():
        pl.semaphore_wait(barrier, devices - 1)
        send(0)

    def later_sums(pair):
        return sum(partial(n, pair, later_ref) for n in range(len(parts)))

    for n in range(len(parts)):
        weigh_piece(n, (later_ref,), 1)
    if turns == 2:
        combine(1, later_sums)

        @pl.when(stn == 0)
        def _():
            pl.semaphore_wait(barrier, devices - 1)
            send(0)

        send(1)
    else:
        @pl.loop(1, turns)
        def _(number):
            @pl.when(number > 1)
            def _():
                channels((number,))

                for n in range(len(parts)):
                    weigh_piece(n, (later_ref,))

            combine(number, later_sums)

            @pl.when((stn == 0) & (number == 1))
            def _():
                pl.semaphore_wait(barrier, devices - 1)
                send(0)

            send(number)

    own = pltpu.make_async_copy(spectra_ref.at[stn], all_ref.at[place], sems.at[4])
    own.start()

    @pl.when(tm < last)
    def _():
        own_tail = pltpu.make_async_copy(tails_ref.at[stn], before_ref.at[place], sems.at[5])
        own_tail.start()
        own_tail.wait()

    order_copy.wait()
    total = stations * inputs
    half = order_ref.shape[1]
    cols = stations * tile
    row = lax.broadcasted_iota(jnp.int32, (total, half), 0)
    at_station = jnp.where(order_ref[...] == row // 2, 1.0, 0.0).astype(jnp.bfloat16)
    col = lax.broadcasted_iota(jnp.int32, (half, cols), 1)
    station = (col // tile) * (inputs // 2) + (col % inputs) // 2
    spread = jnp.where(station == lax.broadcasted_iota(jnp.int32, (half, cols), 0), 1.0, 0.0).astype(jnp.bfloat16)
    chosen = jnp.dot(at_station, spread, preferred_element_type=jnp.float32)
    row = lax.broadcasted_iota(jnp.int32, (total, cols), 0)
    col = lax.broadcasted_iota(jnp.int32, (total, cols), 1)
    chosen = jnp.where(row % 2 == col % 2, chosen, 0.0)
    side = (col // inputs) % 2
    pick = [jnp.where(side == p, chosen, 0.0).astype(jnp.bfloat16) for p in range(2)]

    own.wait()
    others = all_ref.at[pl.ds(0, devices - 1)]

    def moved(ref, sem):
        return pltpu.make_async_remote_copy(
            src_ref=ref,
            dst_ref=ref,
            send_sem=sems.at[sem],
            recv_sem=sems.at[sem + 1],
            device_id=(stn, lax.rem(tm + 1, groups)),
            device_id_type=MESH,
        )

    moved(others, 0).wait_recv()
    slots = last * stations

    @pl.when(tm < last)
    def _():
        moved(before_ref.at[pl.ds(0, slots - 1)], 2).wait_recv()

    @pl.when(tm == last)
    def _():
        moved(before_ref.at[pl.ds(0, slots)], 2).wait_recv()

    for g in range(groups):
        tiles = all_ref[g * stations:(g + 1) * stations].reshape(cols, frames)
        if g > 0:
            tails = before_ref[(g - 1) * stations:g * stations].reshape(2 * stations, 1, frames)
            tails = jnp.broadcast_to(tails, (2 * stations, inputs, frames)).reshape(cols, frames)
            tails = pltpu.roll(tails, 0, axis=1, stride=span, stride_axis=0)
            early = lax.broadcasted_iota(jnp.int32, (cols, frames), 1) < n_taps - 1
            tiles = (tiles.astype(jnp.float32) + jnp.where(early, tails, 0.0)).astype(jnp.bfloat16)
        for p in range(2):
            found = jnp.dot(pick[p], tiles, preferred_element_type=jnp.float32)
            at = p * groups * frames + g * frames
            catalog_ref[0, :, at:at + frames] = found.astype(jnp.bfloat16)
    whole = groups * frames
    catalog_ref[1, :, 0:whole] = catalog_ref[0, :, whole:]
    catalog_ref[1, :, whole:] = -catalog_ref[0, :, 0:whole]
    count = total // groups
    mine = pl.ds(pl.multiple_of(tm * count, count), count)
    scale = 1.0 / whole
    for p in range(2):
        out_ref[:, p, :] = scale * lax.dot_general(
            catalog_ref[p, mine, :], catalog_ref[0], NT, preferred_element_type=jnp.float32
        )
    moved(others, 0).wait_send()

    @pl.when(tm < last)
    def _():
        moved(before_ref.at[pl.ds(0, devices - 1)], 2).wait_send()


def body(voltages, filter_taps, channel_keep, station_order):
    inputs, frames, n_chan = voltages.shape
    n_taps = filter_taps.shape[0]
    n_sub = channel_keep.shape[0]
    half = station_order.shape[0]
    groups = lax.axis_size("tm")
    stations = lax.axis_size("stn")
    total = stations * inputs
    tile = 2 * inputs
    kept = stations
    edges = [0] + [cut for cut in CUTS if cut < n_chan] + [n_chan]
    weights = tuple(
        pltpu.VMEM((2 * GROUP * n_taps, hi - lo), jnp.bfloat16) for lo, hi in zip(edges[:-1], edges[1:])
    )
    arguments = (voltages, filter_taps, channel_keep.reshape(1, n_sub), station_order.reshape(1, half))
    sums = pl.pallas_call(
        functools.partial(fused_kernel, groups=groups, stations=stations),
        in_specs=[pl.BlockSpec(memory_space=pltpu.HBM)] * 4,
        out_specs=pl.BlockSpec(memory_space=pltpu.VMEM),
        out_shape=jax.ShapeDtypeStruct((total // groups, 2, total), jnp.float32),
        scratch_shapes=[
            pltpu.VMEM((inputs, frames, n_chan), jnp.bfloat16),
            pltpu.VMEM((n_taps, n_chan), jnp.float32),
            pltpu.VMEM((1, n_sub), jnp.int32),
            pltpu.VMEM((1, half), jnp.int32),
            pltpu.VMEM((2 * GROUP * n_taps, inputs * frames), jnp.float32),
            pltpu.VMEM((4, 2 * GROUP, WIDE), jnp.float32),
            weights,
            weights,
            pltpu.VMEM((GROUP * tile, frames), jnp.float32),
            pltpu.VMEM((kept, tile, frames), jnp.bfloat16),
            pltpu.VMEM((kept, 2, frames), jnp.float32),
            pltpu.VMEM((groups * stations, tile, frames), jnp.bfloat16),
            pltpu.VMEM((groups * stations, 2, frames), jnp.float32),
            pltpu.VMEM((2, total, 2 * groups * frames), jnp.bfloat16),
            pltpu.SemaphoreType.DMA((6,)),
            pltpu.SemaphoreType.DMA((4 + len(CUTS),)),
        ],
        compiler_params=pltpu.CompilerParams(collective_id=0, has_side_effects=True, vmem_limit_bytes=40 << 20),
    )(*[pltpu.with_memory_space_constraint(x, pltpu.HBM) for x in arguments])
    return sums.reshape(total // groups, 1, 2, total)


def solution(mesh):
    placed = (P("stn", "tm", None), P(), P(), P())
    return jax.shard_map(
        body, mesh=mesh, in_specs=placed, out_specs=P("tm", "stn", None, None), check_vma=False
    )
```

```python
import functools
import math

import jax
import jax.numpy as jnp
from jax import lax
from jax.experimental import pallas as pl
from jax.experimental.pallas import tpu as pltpu
from jax.sharding import PartitionSpec as P

SUB_LO = 1024
GROUP = 8
CHUNK = 512
WIDE = 128
ORDER = ((0, 1, 2, 4, 3, 5, 6, 7), (0, 1, 4, 2, 5, 6, 3, 7))
CUTS = (1024, 2048, 3072)
MESH = pl.DeviceIdType.MESH
NT = (((1,), (1,)), ((), ()))


def fused_kernel(
    volt_hbm, taps_hbm, keep_hbm, order_hbm, out_ref, volt_ref, taps_ref, keep_ref, order_ref,
    acc_ref, base_ref, first_ref, later_ref, main_ref, spectra_ref, tails_ref, all_ref, before_ref, catalog_ref,
    sems, load_sems, *, groups, stations,
):
    inputs, frames, n_chan = volt_ref.shape
    n_taps = taps_ref.shape[0]
    n_sub = keep_ref.shape[1]
    assert n_chan & (n_chan - 1) == 0 and n_chan <= WIDE * WIDE
    unit = 2.0 * math.pi / n_chan
    rows = 2 * GROUP
    turns = stations // GROUP
    span = frames // inputs
    tile = 2 * inputs
    stn = lax.axis_index("stn")
    tm = lax.axis_index("tm")
    devices = groups * stations
    me = stn * groups + tm
    place = tm * stations + stn
    last = groups - 1
    barrier = pltpu.get_barrier_semaphore()
    edges = [0] + [cut for cut in CUTS if cut < n_chan] + [n_chan]
    parts = [slice(lo, hi) for lo, hi in zip(edges[:-1], edges[1:])]

    keep_copy = pltpu.make_async_copy(keep_hbm, keep_ref, load_sems.at[0])
    taps_copy = pltpu.make_async_copy(taps_hbm, taps_ref, load_sems.at[1])
    order_copy = pltpu.make_async_copy(order_hbm, order_ref, load_sems.at[2])
    loads = [
        pltpu.make_async_copy(volt_hbm.at[:, :, part], volt_ref.at[:, :, part], load_sems.at[3 + n])
        for n, part in enumerate(parts)
    ]
    keep_copy.start()
    taps_copy.start()
    for load in loads:
        load.start()
    order_copy.start()

    @pl.loop(1, devices)
    def _(distance):
        device = lax.rem(me + distance, devices)
        pl.semaphore_signal(
            barrier, inc=1, device_id=(device // groups, lax.rem(device, groups)), device_id_type=MESH
        )

    def channels(numbers):
        keep = keep_ref[...]
        before = lax.broadcasted_iota(jnp.int32, (n_sub, n_sub), 0) <= lax.broadcasted_iota(jnp.int32, (n_sub, n_sub), 1)
        count = GROUP * len(numbers)
        keep_rows = jnp.broadcast_to(keep, (count, n_sub))
        rank = jnp.dot(
            keep_rows.astype(jnp.float32).astype(jnp.bfloat16),
            before.astype(jnp.float32).astype(jnp.bfloat16),
            preferred_element_type=jnp.float32,
        )
        slot = jnp.concatenate(
            [lax.broadcasted_iota(jnp.int32, (GROUP, n_sub), 0) + 1 + number * GROUP for number in numbers]
        ).astype(jnp.float32)
        number = lax.broadcasted_iota(jnp.int32, (count, n_sub), 1).astype(jnp.float32)
        hit = jnp.where((rank == slot) & (keep_rows == 1), number, 0.0)
        channel = jnp.sum(hit, axis=1, keepdims=True).astype(jnp.int32) + SUB_LO
        column = lax.broadcasted_iota(jnp.int32, (count, WIDE), 1)
        norm = 1.0 / math.sqrt(n_chan)
        for n, (pace, size) in enumerate(((1, 1.0), (WIDE, norm))):
            angle = ((channel * (column * pace)) & (n_chan - 1)).astype(jnp.float32) * unit
            base_ref[2 * n, 0:count] = jnp.cos(angle) * size
            base_ref[2 * n + 1, 0:count] = jnp.sin(angle) * size

    def weigh(part, targets, skip=0):
        count = GROUP * len(targets)
        lines = slice(skip * GROUP, skip * GROUP + count)
        cos_base, sin_base, cos_all, sin_all = [base_ref[n, lines] for n in range(4)]
        real, imag = [], []
        for block in range(CHUNK // WIDE):
            at = part * (CHUNK // WIDE) + block
            cos_step, sin_step = cos_all[:, at:at + 1], sin_all[:, at:at + 1]
            real.append(cos_step * cos_base - sin_step * sin_base)
            imag.append(-(sin_step * cos_base + cos_step * sin_base))
        real, imag = [jnp.concatenate(blocks, axis=1) for blocks in (real, imag)]
        taps = taps_ref[:, part * CHUNK:(part + 1) * CHUNK]
        held = [n for n, piece in enumerate(parts) if piece.start <= part * CHUNK < piece.stop][0]
        columns = slice(part * CHUNK - parts[held].start, (part + 1) * CHUNK - parts[held].start)
        for n, w_refs in enumerate(targets):
            own = slice(n * GROUP, (n + 1) * GROUP)
            table = jnp.concatenate([real[own], imag[own]], axis=0).astype(jnp.bfloat16).astype(jnp.float32)
            for tap in range(n_taps):
                w_refs[held][tap * rows:(tap + 1) * rows, columns] = (table * taps[tap:tap + 1, :]).astype(jnp.bfloat16)

    lane = lax.broadcasted_iota(jnp.int32, (rows, frames), 1)

    def combine(number, product):
        packed = jnp.zeros((rows, frames), jnp.float32)
        for pair in range(inputs // 4):
            sums = product(pair)
            for half in range(4):
                i = 4 * pair + half
                inside = sums[(n_taps - 1) * rows:, half * frames:(half + 1) * frames]
                beyond = jnp.zeros((rows, frames), jnp.float32)
                for tap in range(n_taps - 1):
                    shift = n_taps - 1 - tap
                    piece = pltpu.roll(sums[tap * rows:(tap + 1) * rows, half * frames:(half + 1) * frames], shift, axis=1)
                    beyond = beyond + jnp.where(lane < shift, piece, 0.0)
                    inside = inside + jnp.where(lane < shift, 0.0, piece)
                for p in range(2):
                    main_ref[pl.ds(p * inputs + i, GROUP, stride=tile), :] = inside[p * GROUP:(p + 1) * GROUP]
                packed = packed + (pltpu.roll(beyond, frames - i * span, axis=1) if i > 0 else beyond)
        first = number * GROUP
        spectra_ref[pl.ds(first, GROUP)] = main_ref[...].astype(jnp.bfloat16).reshape(GROUP, tile, frames)
        for p in range(2):
            tails_ref[pl.ds(first, GROUP), p, :] = packed[p * GROUP:(p + 1) * GROUP]

    def send(number):
        first = number * GROUP

        def to(to_stn, to_tm):
            @pl.when((to_stn != stn) | (to_tm != tm))
            def _():
                pltpu.make_async_remote_copy(
                    src_ref=spectra_ref.at[to_stn],
                    dst_ref=all_ref.at[place],
                    send_sem=sems.at[0],
                    recv_sem=sems.at[1],
                    device_id=(to_stn, to_tm),
                    device_id_type=MESH,
                ).start()

                @pl.when(tm < last)
                def _():
                    pltpu.make_async_remote_copy(
                        src_ref=tails_ref.at[to_stn],
                        dst_ref=before_ref.at[place],
                        send_sem=sems.at[2],
                        recv_sem=sems.at[3],
                        device_id=(to_stn, to_tm),
                        device_id_type=MESH,
                    ).start()

        for chip in ORDER[0 if isinstance(number, int) and number == 0 else 1]:
            for core in range(groups):
                to(first + chip, core)

    keep_copy.wait()
    taps_copy.wait()
    channels((0, 1))
    def weigh_piece(n, targets, skip=0):
        for part in range(parts[n].start // CHUNK, parts[n].stop // CHUNK):
            weigh(part, targets, skip)

    for n in range(len(parts)):
        weigh_piece(n, (first_ref,), 0)

    def partial(n, pair, w_refs):
        volts = volt_ref[4 * pair:4 * pair + 4, :, parts[n]].reshape(4 * frames, parts[n].stop - parts[n].start)
        return lax.dot_general(w_refs[n][...], volts, NT, preferred_element_type=jnp.float32)

    for n in range(len(parts) - 1):
        loads[n].wait()
        for pair in range(inputs // 4):
            found = partial(n, pair, first_ref)
            at = slice(4 * pair * frames, (4 * pair + 4) * frames)
            acc_ref[:, at] = found if n == 0 else acc_ref[:, at] + found

    loads[-1].wait()

    def first_sums(pair):
        return acc_ref[:, 4 * pair * frames:(4 * pair + 4) * frames] + partial(len(parts) - 1, pair, first_ref)

    combine(0, first_sums)

    @pl.when(stn > 0)
    def _():
        pl.semaphore_wait(barrier, devices - 1)
        send(0)

    def later_sums(pair):
        return sum(partial(n, pair, later_ref) for n in range(len(parts)))

    for n in range(len(parts)):
        weigh_piece(n, (later_ref,), 1)
    if turns == 2:
        combine(1, later_sums)

        @pl.when(stn == 0)
        def _():
            pl.semaphore_wait(barrier, devices - 1)
            send(0)

        send(1)
    else:
        @pl.loop(1, turns)
        def _(number):
            @pl.when(number > 1)
            def _():
                channels((number,))

                for n in range(len(parts)):
                    weigh_piece(n, (later_ref,))

            combine(number, later_sums)

            @pl.when((stn == 0) & (number == 1))
            def _():
                pl.semaphore_wait(barrier, devices - 1)
                send(0)

            send(number)

    own = pltpu.make_async_copy(spectra_ref.at[stn], all_ref.at[place], sems.at[4])
    own.start()

    @pl.when(tm < last)
    def _():
        own_tail = pltpu.make_async_copy(tails_ref.at[stn], before_ref.at[place], sems.at[5])
        own_tail.start()
        own_tail.wait()

    order_copy.wait()
    total = stations * inputs
    half = order_ref.shape[1]
    cols = stations * tile
    row = lax.broadcasted_iota(jnp.int32, (total, half), 0)
    at_station = jnp.where(order_ref[...] == row // 2, 1.0, 0.0).astype(jnp.bfloat16)
    col = lax.broadcasted_iota(jnp.int32, (half, cols), 1)
    station = (col // tile) * (inputs // 2) + (col % inputs) // 2
    spread = jnp.where(station == lax.broadcasted_iota(jnp.int32, (half, cols), 0), 1.0, 0.0).astype(jnp.bfloat16)
    chosen = jnp.dot(at_station, spread, preferred_element_type=jnp.float32)
    row = lax.broadcasted_iota(jnp.int32, (total, cols), 0)
    col = lax.broadcasted_iota(jnp.int32, (total, cols), 1)
    chosen = jnp.where(row % 2 == col % 2, chosen, 0.0)
    side = (col // inputs) % 2
    pick = [jnp.where(side == p, chosen, 0.0).astype(jnp.bfloat16) for p in range(2)]

    own.wait()
    others = all_ref.at[pl.ds(0, devices - 1)]

    def moved(ref, sem):
        return pltpu.make_async_remote_copy(
            src_ref=ref,
            dst_ref=ref,
            send_sem=sems.at[sem],
            recv_sem=sems.at[sem + 1],
            device_id=(stn, lax.rem(tm + 1, groups)),
            device_id_type=MESH,
        )

    moved(others, 0).wait_recv()
    slots = last * stations

    @pl.when(tm < last)
    def _():
        moved(before_ref.at[pl.ds(0, slots - 1)], 2).wait_recv()

    @pl.when(tm == last)
    def _():
        moved(before_ref.at[pl.ds(0, slots)], 2).wait_recv()

    for g in range(groups):
        tiles = all_ref[g * stations:(g + 1) * stations].reshape(cols, frames)
        if g > 0:
            tails = before_ref[(g - 1) * stations:g * stations].reshape(2 * stations, 1, frames)
            tails = jnp.broadcast_to(tails, (2 * stations, inputs, frames)).reshape(cols, frames)
            tails = pltpu.roll(tails, 0, axis=1, stride=span, stride_axis=0)
            early = lax.broadcasted_iota(jnp.int32, (cols, frames), 1) < n_taps - 1
            tiles = (tiles.astype(jnp.float32) + jnp.where(early, tails, 0.0)).astype(jnp.bfloat16)
        for p in range(2):
            found = jnp.dot(pick[p], tiles, preferred_element_type=jnp.float32)
            at = p * groups * frames + g * frames
            catalog_ref[0, :, at:at + frames] = found.astype(jnp.bfloat16)
    whole = groups * frames
    catalog_ref[1, :, 0:whole] = catalog_ref[0, :, whole:]
    catalog_ref[1, :, whole:] = -catalog_ref[0, :, 0:whole]
    count = total // groups
    mine = pl.ds(pl.multiple_of(tm * count, count), count)
    scale = 1.0 / whole
    for p in range(2):
        out_ref[:, p, :] = scale * lax.dot_general(
            catalog_ref[p, mine, :], catalog_ref[0], NT, preferred_element_type=jnp.float32
        )
    moved(others, 0).wait_send()

    @pl.when(tm < last)
    def _():
        moved(before_ref.at[pl.ds(0, devices - 1)], 2).wait_send()


def body(voltages, filter_taps, channel_keep, station_order):
    inputs, frames, n_chan = voltages.shape
    n_taps = filter_taps.shape[0]
    n_sub = channel_keep.shape[0]
    half = station_order.shape[0]
    groups = lax.axis_size("tm")
    stations = lax.axis_size("stn")
    total = stations * inputs
    tile = 2 * inputs
    kept = stations
    edges = [0] + [cut for cut in CUTS if cut < n_chan] + [n_chan]
    weights = tuple(
        pltpu.VMEM((2 * GROUP * n_taps, hi - lo), jnp.bfloat16) for lo, hi in zip(edges[:-1], edges[1:])
    )
    arguments = (voltages, filter_taps, channel_keep.reshape(1, n_sub), station_order.reshape(1, half))
    sums = pl.pallas_call(
        functools.partial(fused_kernel, groups=groups, stations=stations),
        in_specs=[pl.BlockSpec(memory_space=pltpu.HBM)] * 4,
        out_specs=pl.BlockSpec(memory_space=pltpu.VMEM),
        out_shape=jax.ShapeDtypeStruct((total // groups, 2, total), jnp.float32),
        scratch_shapes=[
            pltpu.VMEM((inputs, frames, n_chan), jnp.bfloat16),
            pltpu.VMEM((n_taps, n_chan), jnp.float32),
            pltpu.VMEM((1, n_sub), jnp.int32),
            pltpu.VMEM((1, half), jnp.int32),
            pltpu.VMEM((2 * GROUP * n_taps, inputs * frames), jnp.float32),
            pltpu.VMEM((4, 2 * GROUP, WIDE), jnp.float32),
            weights,
            weights,
            pltpu.VMEM((GROUP * tile, frames), jnp.float32),
            pltpu.VMEM((kept, tile, frames), jnp.bfloat16),
            pltpu.VMEM((kept, 2, frames), jnp.float32),
            pltpu.VMEM((groups * stations, tile, frames), jnp.bfloat16),
            pltpu.VMEM((groups * stations, 2, frames), jnp.float32),
            pltpu.VMEM((2, total, 2 * groups * frames), jnp.bfloat16),
            pltpu.SemaphoreType.DMA((6,)),
            pltpu.SemaphoreType.DMA((4 + len(CUTS),)),
        ],
        compiler_params=pltpu.CompilerParams(collective_id=0, has_side_effects=True, vmem_limit_bytes=40 << 20),
    )(*[pltpu.with_memory_space_constraint(x, pltpu.HBM) for x in arguments])
    return sums.reshape(total // groups, 1, 2, total)


def solution(mesh):
    placed = (P("stn", "tm", None), P(), P(), P())
    return jax.shard_map(
        body, mesh=mesh, in_specs=placed, out_specs=P("tm", "stn", None, None), check_vma=False
    )
```
